128 devices in a mesh: period: 16 (over x, y), region: 8 (over z, core).
Axes of the slice: x: 4, y: 4, z: 4, core: 2. Of those that a mesh axis runs over, the one named last changes fastest.
Arguments:
- transition: float32 [128, 256, 128, 128], P('region', 'period'), may hold values from -0.05 to 1, as said below
- forcing: float32 [128, 256, 128], P('region', 'period'), may hold values from -0.8 to 0.8
- terminal: float32 [128, 128], P('region'), may hold values from -6 to 6
- partners: int32 [8, 128, 8], replicated, may hold values from 0 to 127
- shares: float32 [8, 128, 8], replicated, may hold values from 0.02 to 0.2
Outputs:
- costate: float32 [128, 256, 128], P('region', 'period')
- clearing: float32 [128, 256, 128], P(None, ('period', 'region'))
The draws below stay inside these ranges and needn't reach their ends.
Inputs may be any that keep to these rules, and one draw needn't show every extreme that they name: The diagonal entries of each transition block lie from 0.54 to 1.0 and the off-diagonal entries are at most 0.05 in magnitude. `partners`: entries may repeat.
All inputs are finite; a program needn't handle non-finite values.
Results may differ from the reference program's by a relative error of at most 0.00013.
Values sent between devices are 32-bit elements; how exact they have to be, the bound alone decides.
A program may use at most 128 MiB of HBM per device.

```python
import math
import jax
import jax.numpy as jnp
from jax import lax

SECTORS = 128
BLOCKS = 8
PARTNERS = 8
SUB = 16
REGIONS = 128
HORIZON_STEPS = 256


def draw_transition(key, part):
    random_keys = jax.random.split(jax.random.fold_in(key, 11), 5)
    gradual_component = jax.random.uniform(random_keys[0], (REGIONS, 1, SECTORS)) < 0.5
    gradual_decay_rate = jax.random.uniform(random_keys[1], (REGIONS, HORIZON_STEPS, SECTORS), minval=0.993, maxval=1.0)
    quick_decay_rate = jax.random.uniform(random_keys[2], (REGIONS, HORIZON_STEPS, SECTORS), minval=0.9, maxval=0.95)
    shock_impulse = jax.random.uniform(random_keys[3], (1, HORIZON_STEPS, 1)) < 8.0 / HORIZON_STEPS
    diagonal_entries = jnp.where(gradual_component, gradual_decay_rate, quick_decay_rate) * jnp.where(shock_impulse, 0.6, 1.0)
    spread = jax.random.normal(random_keys[4], (REGIONS, HORIZON_STEPS, SECTORS, SECTORS)) * 0.1
    spread = jnp.clip(spread / jnp.sqrt(jnp.float32(SECTORS)), -0.05, 0.05)
    eye = jnp.eye(SECTORS, dtype=jnp.float32)
    return (spread * (1.0 - eye) + diagonal_entries[..., None] * eye).astype(jnp.float32)


def touch_ends(result, own_key, low, high):
    dims = result.shape
    place = [jax.random.randint(jax.random.fold_in(own_key, axis), (), 0, dims[axis]) for axis in range(len(dims))]
    result = result.at[tuple(place)].set(low)
    longest = dims.index(max(dims))
    place[longest] = (place[longest] + 1) % dims[longest]
    return result.at[tuple(place)].set(high)


def shard_levels(key, shape, shards, low, high):
    loudness, own = 1.0, jax.random.fold_in(key, 6)
    for position, blocks in shards:
        heights = jnp.exp(jax.random.uniform(jax.random.fold_in(own, position), (blocks,), jnp.float32, low / len(shards), high / len(shards)))
        loudness = loudness * jnp.repeat(heights, shape[position] // blocks).reshape([-1 if axis == position else 1 for axis in range(len(shape))])
    return loudness


def normal_values(rng, extent, scale, bound, pieces=(), held_as=jnp.bfloat16):
    gain = shard_levels(rng, extent, pieces, -0.22, 0.18) if pieces else 1.0
    drawn = jax.random.normal(rng, extent, jnp.float32) * scale * gain
    return jnp.minimum(jnp.maximum(drawn, -bound), bound).astype(held_as)


def setup_inputs(seed: int = 0) -> dict:
    keys = jax.random.split(jax.random.key(seed), 6)
    return {
        "transition": draw_transition(jax.random.fold_in(keys[5], 71), 0),
        "forcing": normal_values(keys[1], (REGIONS, HORIZON_STEPS, SECTORS), 0.1, 0.8, ((0, 8), (1, 16)), jnp.float32),
        "terminal": normal_values(keys[2], (REGIONS, SECTORS), 1.0, 6.0, ((0, 8),), jnp.float32),
        "partners": touch_ends(jax.random.randint(keys[3], (BLOCKS, REGIONS, PARTNERS), 0, REGIONS), jax.random.fold_in(keys[3], 1), 0, REGIONS - 1).astype(jnp.int32),
        "shares": jnp.clip(jnp.exp(jax.random.uniform(keys[4], (BLOCKS, REGIONS, PARTNERS), jnp.float32, math.log(0.02), math.log(0.2))), 0.02, 0.2),
    }


def reference(transition, forcing, terminal, partners, shares):
    def advance(carry, inputs):
        block, vec = inputs
        nxt = jnp.einsum("rij,rj->ri", block, carry, precision=lax.Precision.HIGHEST) + vec
        return nxt, nxt

    moving = (jnp.swapaxes(transition, 0, 1), jnp.swapaxes(forcing, 0, 1))
    final, states = lax.scan(advance, terminal, moving, reverse=True)
    costate = jnp.swapaxes(states, 0, 1)
    regions = costate.shape[0]
    match = partners[..., None] == jnp.arange(regions, dtype=jnp.int32)
    trade = jnp.sum(jnp.where(match, shares[..., None], jnp.float32(0.0)), axis=2)
    flow = jnp.tanh(costate)
    blocked = flow.reshape(regions, flow.shape[1], BLOCKS, SUB)
    mixed = jnp.einsum("grq,qtgs->rtgs", trade, blocked, precision=lax.Precision.HIGHEST)
    clearing = (blocked - mixed).reshape(costate.shape)
    return costate, clearing
```

```python
import functools

import jax
import jax.numpy as jnp
from jax import lax
from jax.experimental import pallas as pl
from jax.experimental.pallas import tpu as pltpu
from jax.sharding import PartitionSpec as P

BLOCKS = 8
BATCH = 4
NT = (((1,), (1,)), ((), ()))
NN = (((1,), (0,)), ((), ()))
F32 = jnp.float32
BF16 = jnp.bfloat16
MESH = pl.DeviceIdType.MESH


def split(x):
    high = x.astype(BF16)
    return high, (x - high.astype(F32)).astype(BF16)


def dot(left, right, dims):
    return lax.dot_general(left, right, dims, preferred_element_type=F32)


def kernel(
    nper,
    nreg,
    trans_hbm,
    force_hbm,
    term_hbm,
    part_hbm,
    share_hbm,
    costate_hbm,
    clear_hbm,
    maps,
    force,
    term,
    part,
    share,
    offsets,
    left,
    outgoing,
    incoming,
    edges,
    starts,
    costate,
    flow,
    traded,
    mixer,
    clear,
    load_sem,
    small_sem,
    map_send,
    map_recv,
    edge_send,
    edge_recv,
    flow_send,
    flow_recv,
    out_sem,
):
    rows, per, sec = force.shape
    here, zone = lax.axis_index("period"), lax.axis_index("region")
    batches = rows // BATCH
    chunk = per // 4
    share_t = per // nreg
    half = rows // 2

    def base_of(k):
        return lax.rem(lax.div(here, BATCH) + 1 + k, batches) * BATCH

    def load(k, c):
        where = (pl.ds(base_of(k), BATCH), pl.ds(per - chunk * (c + 1), chunk))
        return pltpu.make_async_copy(trans_hbm.at[where], maps.at[where], load_sem.at[k, c])

    small = [
        pltpu.make_async_copy(src, dst, small_sem.at[i])
        for i, (src, dst) in enumerate(
            [(force_hbm, force), (term_hbm, term), (part_hbm, part), (share_hbm, share)]
        )
    ]
    small[0].start()
    for k in range(batches):
        for c in range(4):
            load(k, c).start()
    for copy in small[1:]:
        copy.start()

    barrier = pltpu.get_barrier_semaphore()
    for step in range(1, nper):
        pl.semaphore_signal(
            barrier, inc=1, device_id=(lax.rem(here + step, nper), zone), device_id_type=MESH
        )
    for step in range(1, nreg):
        pl.semaphore_signal(
            barrier, inc=1, device_id=(here, lax.rem(zone + step, nreg)), device_id_type=MESH
        )

    square = (sec, sec)
    eye = lax.broadcasted_iota(jnp.int32, square, 0) == lax.broadcasted_iota(jnp.int32, square, 1)
    top = lax.broadcasted_iota(jnp.int32, (16, sec), 0) == 0

    def send_map(row):
        return pltpu.make_async_remote_copy(
            src_ref=outgoing.at[row],
            dst_ref=incoming.at[here],
            send_sem=map_send.at[row],
            recv_sem=map_recv.at[here],
            device_id=(row, zone),
            device_id_type=MESH,
        )

    def keep_map():
        return pltpu.make_async_copy(outgoing.at[here], incoming.at[here], map_recv.at[here])

    small[0].wait()

    def compose(k, carry):
        base = base_of(k)
        for c in range(4):
            load(k, c).wait()
            for inner in range(chunk):
                t = per - 1 - chunk * c - inner
                for i in range(BATCH):
                    row = base + i
                    block = maps[row, t]
                    source = force[row, t : t + 1]
                    if t == per - 1:
                        prod = block.T
                        offset = jnp.where(top, source, 0.0)
                    else:
                        diag = jnp.sum(jnp.where(eye, block, 0.0), axis=0, keepdims=True)
                        high, low = split(jnp.where(eye, 0.0, block))
                        held = left[i]
                        prod = dot(held, jnp.concatenate([high, high], 1), NT)
                        prod += dot(held[:, :sec], low, NT)
                        offset = prod[sec:] + offsets[row, t + 1 : t + 2] * diag + source
                        offset = jnp.where(top, offset, 0.0)
                        prod = prod[:sec] + maps[row, t + 1] * diag
                    maps[row, t] = prod
                    offsets[row, t : t + 1] = offset[:1]
                    if t > 0:
                        high, low = split(prod)
                        left[i, :sec, :sec] = high
                        left[i, :sec, sec:] = low
                        high, low = split(offset)
                        left[i, sec:, :sec] = high
                        left[i, sec:, sec:] = low
                    else:
                        outgoing[row, :sec] = prod
                        outgoing[row, sec:] = offset[:8]

        @pl.when(k == 0)
        def _():
            pl.semaphore_wait(barrier, nper + nreg - 2)

        for i in range(BATCH):

            @pl.when((base + i != here) & (here != 0))
            def _():
                send_map(base + i).start()

            @pl.when((base + i == here) & (here != 0))
            def _():
                keep_map().start()

        return carry

    lax.fori_loop(0, batches, compose, 0)

    for copy in small[1:]:
        copy.wait()

    region = lax.broadcasted_iota(jnp.int32, square, 0)
    for g in range(BLOCKS):
        ids, amounts = part[g], share[g]
        trade = jnp.zeros(square, F32)
        for j in range(ids.shape[0]):
            trade += jnp.where(ids[j : j + 1] == region, amounts[j : j + 1], 0.0)
        high, low = split(trade.T)
        side = sec * (g % 2)
        mixer[g // 2, :sec, side : side + sec] = high
        mixer[g // 2, sec:, side : side + sec] = low

    def upright(vector):
        return jnp.sum(jnp.where(eye, vector, 0.0), axis=1, keepdims=True)

    def send_edge(p):
        return pltpu.make_async_remote_copy(
            src_ref=edges.at[p],
            dst_ref=starts.at[here],
            send_sem=edge_send.at[p],
            recv_sem=edge_recv.at[here],
            device_id=(p, zone),
            device_id_type=MESH,
        )

    def keep_edge():
        return pltpu.make_async_copy(edges.at[here], starts.at[here], edge_recv.at[here])

    def ship_edge(p):
        @pl.when(p != here)
        def _():
            send_edge(p).start()

        @pl.when(p == here)
        def _():
            keep_edge().start()

    state = term[pl.ds(here, 1), :]
    edges[nper - 1] = state

    def chain(step, state):
        p = nper - 1 - step

        @pl.when(p != here)
        def _():
            pltpu.make_async_remote_copy(
                src_ref=outgoing.at[p],
                dst_ref=incoming.at[p],
                send_sem=map_send.at[p],
                recv_sem=map_recv.at[p],
                device_id=(p, zone),
                device_id_type=MESH,
            ).wait_recv()

        @pl.when(p == here)
        def _():
            keep_map().wait()

        ship_edge(p)
        moved = incoming[p, :sec] * upright(state)
        state = jnp.sum(moved, axis=0, keepdims=True) + incoming[p, sec : sec + 1]
        edges[p - 1] = state
        return state

    lax.fori_loop(0, nper - 1, chain, state)
    ship_edge(0)

    def finish(i, carry):
        row = lax.rem(lax.div(here, half) * half + i, rows)

        @pl.when(row != here)
        def _():
            pltpu.make_async_remote_copy(
                src_ref=edges.at[row],
                dst_ref=starts.at[row],
                send_sem=edge_send.at[row],
                recv_sem=edge_recv.at[row],
                device_id=(row, zone),
                device_id_type=MESH,
            ).wait_recv()

        @pl.when(row == here)
        def _():
            keep_edge().wait()

        column = jnp.broadcast_to(upright(starts[row]), square)
        lines = [jnp.sum(maps[row, t] * column, axis=0, keepdims=True) for t in range(per)]
        value = jnp.concatenate(lines, 0) + offsets[row]
        costate[row] = value
        bent = jnp.tanh(value)
        for t in range(per):
            flow[t, pl.ds(row, 1), :] = bent[t : t + 1]
        return carry

    def send_flow(other, h):
        mine = pl.multiple_of(zone * rows + h * half, 8)
        return pltpu.make_async_remote_copy(
            src_ref=flow.at[pl.ds(other * share_t, share_t), pl.ds(h * half, half)],
            dst_ref=traded.at[:, pl.ds(mine, half)],
            send_sem=flow_send.at[other, h],
            recv_sem=flow_recv.at[zone, h],
            device_id=(here, other),
            device_id_type=MESH,
        )

    def keep_flow(h):
        mine = pl.multiple_of(zone * rows + h * half, 8)
        return pltpu.make_async_copy(
            flow.at[pl.ds(zone * share_t, share_t), pl.ds(h * half, half)],
            traded.at[:, pl.ds(mine, half)],
            flow_recv.at[zone, h],
        )

    def got_flow(other, h):
        theirs = pl.multiple_of(other * rows + h * half, 8)
        return pltpu.make_async_remote_copy(
            src_ref=flow.at[pl.ds(other * share_t, share_t), pl.ds(h * half, half)],
            dst_ref=traded.at[:, pl.ds(theirs, half)],
            send_sem=flow_send.at[other, h],
            recv_sem=flow_recv.at[other, h],
            device_id=(here, other),
            device_id_type=MESH,
        )

    for part_no in range(2):
        lax.fori_loop(part_no * half, (part_no + 1) * half, finish, 0)
        h = lax.rem(lax.div(here, half) + part_no, 2)
        for step in range(1, nreg):
            send_flow(lax.rem(zone + step, nreg), h).start()
        keep_flow(h).start()
    save = pltpu.make_async_copy(costate, costate_hbm, out_sem.at[0])
    save.start()

    for part_no in range(2):
        h = lax.rem(lax.div(here, half) + part_no, 2)
        for step in range(1, nreg):
            got_flow(lax.rem(zone + step, nreg), h).wait_recv()
        keep_flow(h).wait()

    width = share_t * sec
    whole = jnp.concatenate([traded[t] for t in range(share_t)], 1)
    high, low = split(whole)
    group = lax.div(
        lax.rem(lax.broadcasted_iota(jnp.int32, (1, width), 1), sec), sec // BLOCKS
    )
    mixed = jnp.zeros((sec, width), F32)
    for pair in range(BLOCKS // 2):
        masks = [group == 2 * pair, group == 2 * pair + 1]
        tall_high = jnp.concatenate([jnp.where(m, high, BF16(0)) for m in masks], 0)
        tall_low = jnp.concatenate([jnp.where(m, low, BF16(0)) for m in masks], 0)
        first = dot(mixer[pair], tall_high, NN)
        mixed += first[:sec] + first[sec:]
        mixed += dot(mixer[pair, :sec], tall_low, NN)
    result = whole - mixed
    for t in range(share_t):
        clear[t] = result[:, t * sec : (t + 1) * sec]
    done = pltpu.make_async_copy(clear, clear_hbm, out_sem.at[1])
    done.start()

    def drain(row, carry):
        @pl.when(row != here)
        def _():
            send_edge(row).wait_send()

        @pl.when((row != here) & (here != 0))
        def _():
            send_map(row).wait_send()

        return carry

    lax.fori_loop(0, rows, drain, 0)

    for step in range(1, nreg):
        for h in range(2):
            send_flow(lax.rem(zone + step, nreg), h).wait_send()
    save.wait()
    done.wait()


def shards(nper, nreg, transition, forcing, terminal, partners, shares):
    rows, per, sec = forcing.shape
    regions = partners.shape[1]
    share_t = per // nreg
    ids, amounts = jnp.swapaxes(partners, 1, 2), jnp.swapaxes(shares, 1, 2)
    anywhere = pl.BlockSpec(memory_space=pl.ANY)
    dma = pltpu.SemaphoreType.DMA
    costate, clearing = pl.pallas_call(
        functools.partial(kernel, nper, nreg),
        out_shape=(
            jax.ShapeDtypeStruct((rows, per, sec), F32),
            jax.ShapeDtypeStruct((share_t, regions, sec), F32),
        ),
        in_specs=[anywhere] * 5,
        out_specs=[anywhere] * 2,
        scratch_shapes=[
            pltpu.VMEM((rows, per, sec, sec), F32),
            pltpu.VMEM((rows, per, sec), F32),
            pltpu.VMEM((rows, sec), F32),
            pltpu.VMEM(ids.shape, jnp.int32),
            pltpu.VMEM(amounts.shape, F32),
            pltpu.VMEM((rows, per, sec), F32),
            pltpu.VMEM((BATCH, sec + 16, 2 * sec), BF16),
            pltpu.VMEM((rows, sec + 8, sec), F32),
            pltpu.VMEM((nper, sec + 8, sec), F32),
            pltpu.VMEM((nper, 1, sec), F32),
            pltpu.VMEM((rows, 1, sec), F32),
            pltpu.VMEM((rows, per, sec), F32),
            pltpu.VMEM((per, rows, sec), F32),
            pltpu.VMEM((share_t, regions, sec), F32),
            pltpu.VMEM((BLOCKS // 2, 2 * regions, 2 * regions), BF16),
            pltpu.VMEM((share_t, regions, sec), F32),
            dma((rows // BATCH, 4)),
            dma((4,)),
            dma((rows,)),
            dma((nper,)),
            dma((nper,)),
            dma((rows,)),
            dma((nreg, 2)),
            dma((nreg, 2)),
            dma((2,)),
        ],
        compiler_params=pltpu.CompilerParams(
            collective_id=0, has_side_effects=True, vmem_limit_bytes=60 * 2**20
        ),
        name="newton_step",
    )(transition, forcing, terminal, ids, amounts)
    return costate, jnp.swapaxes(clearing, 0, 1)


def solution(mesh):
    return jax.shard_map(
        functools.partial(shards, mesh.shape["period"], mesh.shape["region"]),
        mesh=mesh,
        in_specs=(
            P("region", "period", None, None),
            P("region", "period", None),
            P("region", None),
            P(),
            P(),
        ),
        out_specs=(P("region", "period", None), P(None, ("period", "region"), None)),
        check_vma=False,
    )
```

```python
import functools

import jax
import jax.numpy as jnp
from jax import lax
from jax.experimental import pallas as pl
from jax.experimental.pallas import tpu as pltpu
from jax.sharding import PartitionSpec as P

BLOCKS = 8
BATCH = 4
NT = (((1,), (1,)), ((), ()))
NN = (((1,), (0,)), ((), ()))
F32 = jnp.float32
BF16 = jnp.bfloat16
MESH = pl.DeviceIdType.MESH


def split(x):
    high = x.astype(BF16)
    return high, (x - high.astype(F32)).astype(BF16)


def dot(left, right, dims):
    return lax.dot_general(left, right, dims, preferred_element_type=F32)


def kernel(
    nper,
    nreg,
    trans_hbm,
    force_hbm,
    term_hbm,
    part_hbm,
    share_hbm,
    costate_hbm,
    clear_hbm,
    maps,
    force,
    term,
    part,
    share,
    offsets,
    outgoing,
    incoming,
    edges,
    starts,
    costate,
    flow,
    traded,
    mixer,
    clear,
    load_sem,
    small_sem,
    map_send,
    map_recv,
    edge_send,
    edge_recv,
    flow_send,
    flow_recv,
    out_sem,
):
    rows, per, sec = force.shape
    here, zone = lax.axis_index("period"), lax.axis_index("region")
    batches = rows // BATCH
    chunk = per // 4
    share_t = per // nreg
    half = rows // 2

    def row_of(k, i):
        skew = k + lax.div(k, 2) * (1 - 2 * lax.rem(k, 2))
        along_x = lax.rem(lax.div(here, BATCH) + i, batches)
        return along_x * BATCH + lax.rem(here + i + skew, BATCH)

    def slot_of(row):
        i = lax.rem(lax.div(row, BATCH) + batches - lax.div(here, BATCH), batches)
        skew = lax.rem(row + 2 * BATCH - lax.rem(here, BATCH) - i, BATCH)
        k = skew + lax.div(skew, 2) * (1 - 2 * lax.rem(skew, 2))
        return k * BATCH + i

    def load(k, c, i):
        when = pl.ds(per - chunk * (c + 1), chunk)
        return pltpu.make_async_copy(
            trans_hbm.at[row_of(k, i), when], maps.at[k * BATCH + i, when], load_sem.at[k, c, i]
        )

    small = [
        pltpu.make_async_copy(src, dst, small_sem.at[i])
        for i, (src, dst) in enumerate(
            [(force_hbm, force), (term_hbm, term), (part_hbm, part), (share_hbm, share)]
        )
    ]
    small[0].start()
    for k in range(batches):
        for c in range(4):
            for i in range(BATCH):
                load(k, c, i).start()
    for copy in small[1:]:
        copy.start()

    barrier = pltpu.get_barrier_semaphore()
    for step in range(1, nper):
        pl.semaphore_signal(
            barrier, inc=1, device_id=(lax.rem(here + step, nper), zone), device_id_type=MESH
        )
    for step in range(1, nreg):
        pl.semaphore_signal(
            barrier, inc=1, device_id=(here, lax.rem(zone + step, nreg)), device_id_type=MESH
        )

    square = (sec, sec)
    eye = lax.broadcasted_iota(jnp.int32, square, 0) == lax.broadcasted_iota(jnp.int32, square, 1)
    top = lax.broadcasted_iota(jnp.int32, (16, sec), 0) == 0

    def send_map(k, i):
        row, slot = row_of(k, i), k * BATCH + i
        return pltpu.make_async_remote_copy(
            src_ref=outgoing.at[slot],
            dst_ref=incoming.at[here],
            send_sem=map_send.at[slot],
            recv_sem=map_recv.at[here],
            device_id=(row, zone),
            device_id_type=MESH,
        )

    def keep_map():
        return pltpu.make_async_copy(outgoing.at[0], incoming.at[here], map_recv.at[here])

    small[0].wait()

    def compose(k, carry):
        for c in range(4):
            for i in range(BATCH):
                load(k, c, i).wait()
            for inner in range(chunk):
                t = per - 1 - chunk * c - inner
                for i in range(BATCH):
                    row, slot = row_of(k, i), k * BATCH + i
                    block = maps[slot, t]
                    source = force[row, t : t + 1]
                    if t == per - 1:
                        prod = block.T
                        offset = jnp.broadcast_to(source, (8, sec))
                    else:
                        diag = jnp.sum(jnp.where(eye, block, 0.0), axis=0, keepdims=True)
                        high, low = split(jnp.where(eye, 0.0, block))
                        late, late_offset = maps[slot, t + 1], offsets[slot, t + 1 : t + 2]
                        late_high, late_low = split(late)
                        tail_high, tail_low = split(jnp.where(top, late_offset, 0.0))
                        tall_high = jnp.concatenate([late_high, tail_high], 0)
                        tall_low = jnp.concatenate([late_low, tail_low], 0)
                        prod = dot(
                            jnp.concatenate([tall_high, tall_low, tall_high], 1),
                            jnp.concatenate([high, high, low], 1),
                            NT,
                        )
                        offset = prod[sec : sec + 8] + late_offset * diag + source
                        prod = prod[:sec] + late * diag
                    maps[slot, t] = prod
                    offsets[slot, t : t + 1] = offset[:1]
                    if t == 0:
                        outgoing[slot, :sec] = prod
                        outgoing[slot, sec:] = offset

        @pl.when(k == 0)
        def _():
            pl.semaphore_wait(barrier, nper + nreg - 2)

        for i in (2, 1, 3, 0):
            row = row_of(k, i)

            @pl.when((row != here) & (here != 0))
            def _(i=i):
                send_map(k, i).start()

            @pl.when((row == here) & (here != 0))
            def _():
                keep_map().start()

        return carry

    lax.fori_loop(0, batches, compose, 0)

    for copy in small[1:]:
        copy.wait()

    region = lax.broadcasted_iota(jnp.int32, square, 0)
    for g in range(BLOCKS):
        ids, amounts = part[g], share[g]
        trade = jnp.zeros(square, F32)
        for j in range(ids.shape[0]):
            trade += jnp.where(ids[j : j + 1] == region, amounts[j : j + 1], 0.0)
        high, low = split(trade.T)
        side = sec * (g % 2)
        mixer[g // 2, :sec, side : side + sec] = high
        mixer[g // 2, sec:, side : side + sec] = low

    def upright(vector):
        return jnp.sum(jnp.where(eye, vector, 0.0), axis=1, keepdims=True)

    def send_edge(p):
        return pltpu.make_async_remote_copy(
            src_ref=edges.at[p],
            dst_ref=starts.at[here],
            send_sem=edge_send.at[p],
            recv_sem=edge_recv.at[here],
            device_id=(p, zone),
            device_id_type=MESH,
        )

    def keep_edge():
        return pltpu.make_async_copy(edges.at[here], starts.at[here], edge_recv.at[here])

    def ship_edge(p):
        @pl.when(p != here)
        def _():
            send_edge(p).start()

        @pl.when(p == here)
        def _():
            keep_edge().start()

    state = term[pl.ds(here, 1), :]
    edges[nper - 1] = state

    def chain(step, state):
        p = nper - 1 - step

        @pl.when(p != here)
        def _():
            pltpu.make_async_remote_copy(
                src_ref=outgoing.at[p],
                dst_ref=incoming.at[p],
                send_sem=map_send.at[p],
                recv_sem=map_recv.at[p],
                device_id=(p, zone),
                device_id_type=MESH,
            ).wait_recv()

        @pl.when(p == here)
        def _():
            keep_map().wait()

        ship_edge(p)
        moved = incoming[p, :sec] * upright(state)
        state = jnp.sum(moved, axis=0, keepdims=True) + incoming[p, sec : sec + 1]
        edges[p - 1] = state
        return state

    lax.fori_loop(0, nper - 1, chain, state)
    ship_edge(0)

    def finish(i, carry):
        row = lax.rem(lax.div(here, half) * half + i, rows)
        slot = slot_of(row)

        @pl.when(row != here)
        def _():
            pltpu.make_async_remote_copy(
                src_ref=edges.at[row],
                dst_ref=starts.at[row],
                send_sem=edge_send.at[row],
                recv_sem=edge_recv.at[row],
                device_id=(row, zone),
                device_id_type=MESH,
            ).wait_recv()

        @pl.when(row == here)
        def _():
            keep_edge().wait()

        column = jnp.broadcast_to(upright(starts[row]), square)
        lines = [jnp.sum(maps[slot, t] * column, axis=0, keepdims=True) for t in range(per)]
        value = jnp.concatenate(lines, 0) + offsets[slot]
        costate[row] = value
        bent = jnp.tanh(value)
        for t in range(per):
            flow[t, pl.ds(row, 1), :] = bent[t : t + 1]
        return carry

    def send_flow(other, h):
        mine = pl.multiple_of(zone * rows + h * half, 8)
        return pltpu.make_async_remote_copy(
            src_ref=flow.at[pl.ds(other * share_t, share_t), pl.ds(h * half, half)],
            dst_ref=traded.at[:, pl.ds(mine, half)],
            send_sem=flow_send.at[other, h],
            recv_sem=flow_recv.at[zone, h],
            device_id=(here, other),
            device_id_type=MESH,
        )

    def keep_flow(h):
        mine = pl.multiple_of(zone * rows + h * half, 8)
        return pltpu.make_async_copy(
            flow.at[pl.ds(zone * share_t, share_t), pl.ds(h * half, half)],
            traded.at[:, pl.ds(mine, half)],
            flow_recv.at[zone, h],
        )

    def got_flow(other, h):
        theirs = pl.multiple_of(other * rows + h * half, 8)
        return pltpu.make_async_remote_copy(
            src_ref=flow.at[pl.ds(other * share_t, share_t), pl.ds(h * half, half)],
            dst_ref=traded.at[:, pl.ds(theirs, half)],
            send_sem=flow_send.at[other, h],
            recv_sem=flow_recv.at[other, h],
            device_id=(here, other),
            device_id_type=MESH,
        )

    for part_no in range(2):
        lax.fori_loop(part_no * half, (part_no + 1) * half, finish, 0)
        h = lax.rem(lax.div(here, half) + part_no, 2)
        for step in range(1, nreg):
            send_flow(lax.rem(zone + step, nreg), h).start()
        keep_flow(h).start()
    save = pltpu.make_async_copy(costate, costate_hbm, out_sem.at[0])
    save.start()

    for part_no in range(2):
        h = lax.rem(lax.div(here, half) + part_no, 2)
        for step in range(1, nreg):
            got_flow(lax.rem(zone + step, nreg), h).wait_recv()
        keep_flow(h).wait()

    width = share_t * sec
    whole = jnp.concatenate([traded[t] for t in range(share_t)], 1)
    high, low = split(whole)
    group = lax.div(
        lax.rem(lax.broadcasted_iota(jnp.int32, (1, width), 1), sec), sec // BLOCKS
    )
    mixed = jnp.zeros((sec, width), F32)
    for pair in range(BLOCKS // 2):
        masks = [group == 2 * pair, group == 2 * pair + 1]
        tall_high = jnp.concatenate([jnp.where(m, high, BF16(0)) for m in masks], 0)
        tall_low = jnp.concatenate([jnp.where(m, low, BF16(0)) for m in masks], 0)
        first = dot(mixer[pair], tall_high, NN)
        mixed += first[:sec] + first[sec:]
        mixed += dot(mixer[pair, :sec], tall_low, NN)
    result = whole - mixed
    for t in range(share_t):
        clear[t] = result[:, t * sec : (t + 1) * sec]
    done = pltpu.make_async_copy(clear, clear_hbm, out_sem.at[1])
    done.start()

    def drain(row, carry):
        @pl.when(row != here)
        def _():
            send_edge(row).wait_send()

        @pl.when((row > 0) & (here != 0))
        def _():
            send_map(lax.div(row, BATCH), lax.rem(row, BATCH)).wait_send()

        return carry

    lax.fori_loop(0, rows, drain, 0)

    for step in range(1, nreg):
        for h in range(2):
            send_flow(lax.rem(zone + step, nreg), h).wait_send()
    save.wait()
    done.wait()


def shards(nper, nreg, transition, forcing, terminal, partners, shares):
    rows, per, sec = forcing.shape
    regions = partners.shape[1]
    share_t = per // nreg
    ids, amounts = jnp.swapaxes(partners, 1, 2), jnp.swapaxes(shares, 1, 2)
    anywhere = pl.BlockSpec(memory_space=pl.ANY)
    dma = pltpu.SemaphoreType.DMA
    costate, clearing = pl.pallas_call(
        functools.partial(kernel, nper, nreg),
        out_shape=(
            jax.ShapeDtypeStruct((rows, per, sec), F32),
            jax.ShapeDtypeStruct((share_t, regions, sec), F32),
        ),
        in_specs=[anywhere] * 5,
        out_specs=[anywhere] * 2,
        scratch_shapes=[
            pltpu.VMEM((rows, per, sec, sec), F32),
            pltpu.VMEM((rows, per, sec), F32),
            pltpu.VMEM((rows, sec), F32),
            pltpu.VMEM(ids.shape, jnp.int32),
            pltpu.VMEM(amounts.shape, F32),
            pltpu.VMEM((rows, per, sec), F32),
            pltpu.VMEM((rows, sec + 8, sec), F32),
            pltpu.VMEM((nper, sec + 8, sec), F32),
            pltpu.VMEM((nper, 1, sec), F32),
            pltpu.VMEM((rows, 1, sec), F32),
            pltpu.VMEM((rows, per, sec), F32),
            pltpu.VMEM((per, rows, sec), F32),
            pltpu.VMEM((share_t, regions, sec), F32),
            pltpu.VMEM((BLOCKS // 2, 2 * regions, 2 * regions), BF16),
            pltpu.VMEM((share_t, regions, sec), F32),
            dma((rows // BATCH, 4, BATCH)),
            dma((4,)),
            dma((rows,)),
            dma((nper,)),
            dma((nper,)),
            dma((rows,)),
            dma((nreg, 2)),
            dma((nreg, 2)),
            dma((2,)),
        ],
        compiler_params=pltpu.CompilerParams(
            collective_id=0, has_side_effects=True, vmem_limit_bytes=60 * 2**20
        ),
        name="newton_step",
    )(transition, forcing, terminal, ids, amounts)
    return costate, jnp.swapaxes(clearing, 0, 1)


def solution(mesh):
    return jax.shard_map(
        functools.partial(shards, mesh.shape["period"], mesh.shape["region"]),
        mesh=mesh,
        in_specs=(
            P("region", "period", None, None),
            P("region", "period", None),
            P("region", None),
            P(),
            P(),
        ),
        out_specs=(P("region", "period", None), P(None, ("period", "region"), None)),
        check_vma=False,
    )
```

```python
import functools

import jax
import jax.numpy as jnp
from jax import lax
from jax.experimental import pallas as pl
from jax.experimental.pallas import tpu as pltpu
from jax.sharding import PartitionSpec as P

BLOCKS = 8
BATCH = 4
NT = (((1,), (1,)), ((), ()))
NN = (((1,), (0,)), ((), ()))
F32 = jnp.float32
BF16 = jnp.bfloat16
MESH = pl.DeviceIdType.MESH


def split(x):
    high = x.astype(BF16)
    return high, (x - high.astype(F32)).astype(BF16)


def dot(left, right, dims):
    return lax.dot_general(left, right, dims, preferred_element_type=F32)


def kernel(
    nper,
    nreg,
    trans_hbm,
    force_hbm,
    term_hbm,
    part_hbm,
    share_hbm,
    costate,
    clear,
    maps,
    force,
    term,
    part,
    share,
    offsets,
    unit,
    outgoing,
    incoming,
    edges,
    starts,
    flow,
    traded,
    mixer,
    load_sem,
    small_sem,
    map_send,
    map_recv,
    edge_send,
    edge_recv,
    flow_send,
    flow_recv,
):
    rows, per, sec = force.shape
    here, zone = lax.axis_index("period"), lax.axis_index("region")
    batches = rows // BATCH
    chunk = per // 4
    share_t = per // nreg
    half = rows // 2

    def row_of(k, i):
        skew = k + lax.div(k, 2) * (1 - 2 * lax.rem(k, 2))
        along_x = lax.rem(lax.div(here, BATCH) + i, batches)
        return along_x * BATCH + lax.rem(here + i + skew, BATCH)

    def slot_of(row):
        i = lax.rem(lax.div(row, BATCH) + batches - lax.div(here, BATCH), batches)
        skew = lax.rem(row + 2 * BATCH - lax.rem(here, BATCH) - i, BATCH)
        k = skew + lax.div(skew, 2) * (1 - 2 * lax.rem(skew, 2))
        return k * BATCH + i

    def load(k, c, i):
        when = pl.ds(per - chunk * (c + 1), chunk)
        return pltpu.make_async_copy(
            trans_hbm.at[row_of(k, i), when], maps.at[k * BATCH + i, when], load_sem.at[k, c, i]
        )

    small = [
        pltpu.make_async_copy(src, dst, small_sem.at[i])
        for i, (src, dst) in enumerate(
            [(force_hbm, force), (term_hbm, term), (part_hbm, part), (share_hbm, share)]
        )
    ]
    small[0].start()
    for c in range(4):
        for i in range(BATCH):
            load(0, c, i).start()
    for copy in small[1:]:
        copy.start()

    barrier = pltpu.get_barrier_semaphore()
    for step in range(1, nper):
        pl.semaphore_signal(
            barrier, inc=1, device_id=(lax.rem(here + step, nper), zone), device_id_type=MESH
        )
    for step in range(1, nreg):
        pl.semaphore_signal(
            barrier, inc=1, device_id=(here, lax.rem(zone + step, nreg)), device_id_type=MESH
        )

    square = (sec, sec)
    eye = lax.broadcasted_iota(jnp.int32, square, 0) == lax.broadcasted_iota(jnp.int32, square, 1)
    unit[...] = jnp.where(eye, 1.0, 0.0)
    top = lax.broadcasted_iota(jnp.int32, (16, sec), 0) == 0

    def send_map(k, i):
        row, slot = row_of(k, i), k * BATCH + i
        return pltpu.make_async_remote_copy(
            src_ref=outgoing.at[slot],
            dst_ref=incoming.at[here],
            send_sem=map_send.at[slot],
            recv_sem=map_recv.at[here],
            device_id=(row, zone),
            device_id_type=MESH,
        )

    def keep_map():
        return pltpu.make_async_copy(outgoing.at[0], incoming.at[here], map_recv.at[here])

    small[0].wait()

    def compose(k, carry):
        @pl.when(k < batches - 1)
        def _():
            for c in range(4):
                for i in range(BATCH):
                    load(k + 1, c, i).start()

        for c in range(4):
            for i in range(BATCH):
                load(k, c, i).wait()
            for inner in range(chunk):
                t = per - 1 - chunk * c - inner
                for i in range(BATCH):
                    row, slot = row_of(k, i), k * BATCH + i
                    block = maps[slot, t]
                    source = force[row, t : t + 1]
                    if t == per - 1:
                        prod = block.T
                        offset = jnp.broadcast_to(source, (8, sec))
                    else:
                        high, low = split(block - unit[...])
                        late, late_offset = maps[slot, t + 1], offsets[slot, t + 1 : t + 2]
                        late_high, late_low = split(late)
                        tail_high, tail_low = split(jnp.where(top, late_offset, 0.0))
                        tall_high = jnp.concatenate([late_high, tail_high], 0)
                        tall_low = jnp.concatenate([late_low, tail_low], 0)
                        prod = dot(
                            jnp.concatenate([tall_high, tall_low, tall_high], 1),
                            jnp.concatenate([high, high, low], 1),
                            NT,
                        )
                        offset = prod[sec : sec + 8] + late_offset + source
                        prod = prod[:sec] + late
                    maps[slot, t] = prod
                    offsets[slot, t : t + 1] = offset[:1]
                    if t == 0:
                        outgoing[slot, :sec] = prod
                        outgoing[slot, sec:] = offset

        @pl.when(k == 0)
        def _():
            pl.semaphore_wait(barrier, nper + nreg - 2)

        for i in (2, 1, 3, 0):
            row = row_of(k, i)

            @pl.when((row != here) & (here != 0))
            def _(i=i):
                send_map(k, i).start()

            @pl.when((row == here) & (here != 0))
            def _():
                keep_map().start()

        return carry

    lax.fori_loop(0, batches, compose, 0)

    for copy in small[1:]:
        copy.wait()

    region = lax.broadcasted_iota(jnp.int32, square, 0)
    for g in range(BLOCKS):
        ids, amounts = part[g], share[g]
        trade = jnp.zeros(square, F32)
        for j in range(ids.shape[0]):
            trade += jnp.where(ids[j : j + 1] == region, amounts[j : j + 1], 0.0)
        high, low = split(trade.T)
        side = sec * (g % 2)
        mixer[g // 2, :sec, side : side + sec] = high
        mixer[g // 2, sec:, side : side + sec] = low

    def upright(vector):
        return jnp.sum(jnp.where(eye, vector, 0.0), axis=1, keepdims=True)

    def send_edge(p):
        return pltpu.make_async_remote_copy(
            src_ref=edges.at[p],
            dst_ref=starts.at[here],
            send_sem=edge_send.at[p],
            recv_sem=edge_recv.at[here],
            device_id=(p, zone),
            device_id_type=MESH,
        )

    def keep_edge():
        return pltpu.make_async_copy(edges.at[here], starts.at[here], edge_recv.at[here])

    def ship_edge(p):
        @pl.when(p != here)
        def _():
            send_edge(p).start()

        @pl.when(p == here)
        def _():
            keep_edge().start()

    state = term[pl.ds(here, 1), :]
    edges[nper - 1] = state

    def chain(step, state):
        p = nper - 1 - step

        @pl.when(p != here)
        def _():
            pltpu.make_async_remote_copy(
                src_ref=outgoing.at[p],
                dst_ref=incoming.at[p],
                send_sem=map_send.at[p],
                recv_sem=map_recv.at[p],
                device_id=(p, zone),
                device_id_type=MESH,
            ).wait_recv()

        @pl.when(p == here)
        def _():
            keep_map().wait()

        ship_edge(p)
        moved = incoming[p, :sec] * upright(state)
        state = jnp.sum(moved, axis=0, keepdims=True) + incoming[p, sec : sec + 1]
        edges[p - 1] = state
        return state

    lax.fori_loop(0, nper - 1, chain, state)
    ship_edge(0)

    def finish(i, carry):
        row = lax.rem(lax.div(here, half) * half + i, rows)
        slot = slot_of(row)

        @pl.when(row != here)
        def _():
            pltpu.make_async_remote_copy(
                src_ref=edges.at[row],
                dst_ref=starts.at[row],
                send_sem=edge_send.at[row],
                recv_sem=edge_recv.at[row],
                device_id=(row, zone),
                device_id_type=MESH,
            ).wait_recv()

        @pl.when(row == here)
        def _():
            keep_edge().wait()

        column = jnp.broadcast_to(upright(starts[row]), square)
        lines = [jnp.sum(maps[slot, t] * column, axis=0, keepdims=True) for t in range(per)]
        value = jnp.concatenate(lines, 0) + offsets[slot]
        costate[row] = value
        bent = jnp.tanh(value)
        for t in range(per):
            flow[t, pl.ds(row, 1), :] = bent[t : t + 1]
        return carry

    def send_flow(other, h):
        mine = pl.multiple_of(zone * rows + h * half, 8)
        return pltpu.make_async_remote_copy(
            src_ref=flow.at[pl.ds(other * share_t, share_t), pl.ds(h * half, half)],
            dst_ref=traded.at[:, pl.ds(mine, half)],
            send_sem=flow_send.at[other, h],
            recv_sem=flow_recv.at[zone, h],
            device_id=(here, other),
            device_id_type=MESH,
        )

    def keep_flow(h):
        mine = pl.multiple_of(zone * rows + h * half, 8)
        return pltpu.make_async_copy(
            flow.at[pl.ds(zone * share_t, share_t), pl.ds(h * half, half)],
            traded.at[:, pl.ds(mine, half)],
            flow_recv.at[zone, h],
        )

    def got_flow(other, h):
        theirs = pl.multiple_of(other * rows + h * half, 8)
        return pltpu.make_async_remote_copy(
            src_ref=flow.at[pl.ds(other * share_t, share_t), pl.ds(h * half, half)],
            dst_ref=traded.at[:, pl.ds(theirs, half)],
            send_sem=flow_send.at[other, h],
            recv_sem=flow_recv.at[other, h],
            device_id=(here, other),
            device_id_type=MESH,
        )

    for part_no in range(2):
        lax.fori_loop(part_no * half, (part_no + 1) * half, finish, 0)
        h = lax.rem(lax.div(here, half) + part_no, 2)
        for step in range(1, nreg):
            send_flow(lax.rem(zone + step, nreg), h).start()
        keep_flow(h).start()

    for part_no in range(2):
        h = lax.rem(lax.div(here, half) + part_no, 2)
        for step in range(1, nreg):
            got_flow(lax.rem(zone + step, nreg), h).wait_recv()
        keep_flow(h).wait()

    width = share_t * sec
    whole = jnp.concatenate([traded[t] for t in range(share_t)], 1)
    high, low = split(whole)
    group = lax.div(
        lax.rem(lax.broadcasted_iota(jnp.int32, (1, width), 1), sec), sec // BLOCKS
    )
    mixed = jnp.zeros((sec, width), F32)
    for pair in range(BLOCKS // 2):
        masks = [group == 2 * pair, group == 2 * pair + 1]
        tall_high = jnp.concatenate([jnp.where(m, high, BF16(0)) for m in masks], 0)
        tall_low = jnp.concatenate([jnp.where(m, low, BF16(0)) for m in masks], 0)
        first = dot(mixer[pair], tall_high, NN)
        mixed += first[:sec] + first[sec:]
        mixed += dot(mixer[pair, :sec], tall_low, NN)
    result = whole - mixed
    for t in range(share_t):
        clear[t] = result[:, t * sec : (t + 1) * sec]

    def drain(row, carry):
        @pl.when(row != here)
        def _():
            send_edge(row).wait_send()

        @pl.when((row > 0) & (here != 0))
        def _():
            send_map(lax.div(row, BATCH), lax.rem(row, BATCH)).wait_send()

        return carry

    lax.fori_loop(0, rows, drain, 0)

    for step in range(1, nreg):
        for h in range(2):
            send_flow(lax.rem(zone + step, nreg), h).wait_send()


def shards(nper, nreg, transition, forcing, terminal, partners, shares):
    rows, per, sec = forcing.shape
    regions = partners.shape[1]
    share_t = per // nreg
    ids, amounts = jnp.swapaxes(partners, 1, 2), jnp.swapaxes(shares, 1, 2)
    anywhere = pl.BlockSpec(memory_space=pl.ANY)
    dma = pltpu.SemaphoreType.DMA
    costate, clearing = pl.pallas_call(
        functools.partial(kernel, nper, nreg),
        out_shape=(
            pltpu.VMEM((rows, per, sec), F32),
            pltpu.VMEM((share_t, regions, sec), F32),
        ),
        in_specs=[anywhere] * 5,
        out_specs=[pl.BlockSpec(memory_space=pltpu.VMEM)] * 2,
        scratch_shapes=[
            pltpu.VMEM((rows, per, sec, sec), F32),
            pltpu.VMEM((rows, per, sec), F32),
            pltpu.VMEM((rows, sec), F32),
            pltpu.VMEM(ids.shape, jnp.int32),
            pltpu.VMEM(amounts.shape, F32),
            pltpu.VMEM((rows, per, sec), F32),
            pltpu.VMEM((sec, sec), F32),
            pltpu.VMEM((rows, sec + 8, sec), F32),
            pltpu.VMEM((nper, sec + 8, sec), F32),
            pltpu.VMEM((nper, 1, sec), F32),
            pltpu.VMEM((rows, 1, sec), F32),
            pltpu.VMEM((per, rows, sec), F32),
            pltpu.VMEM((share_t, regions, sec), F32),
            pltpu.VMEM((BLOCKS // 2, 2 * regions, 2 * regions), BF16),
            dma((rows // BATCH, 4, BATCH)),
            dma((4,)),
            dma((rows,)),
            dma((nper,)),
            dma((nper,)),
            dma((rows,)),
            dma((nreg, 2)),
            dma((nreg, 2)),
        ],
        compiler_params=pltpu.CompilerParams(
            collective_id=0, has_side_effects=True, vmem_limit_bytes=60 * 2**20
        ),
        name="newton_step",
    )(transition, forcing, terminal, ids, amounts)
    return costate, jnp.swapaxes(clearing, 0, 1)


def solution(mesh):
    return jax.shard_map(
        functools.partial(shards, mesh.shape["period"], mesh.shape["region"]),
        mesh=mesh,
        in_specs=(
            P("region", "period", None, None),
            P("region", "period", None),
            P("region", None),
            P(),
            P(),
        ),
        out_specs=(P("region", "period", None), P(None, ("period", "region"), None)),
        check_vma=False,
    )
```

```python
import functools

import jax
import jax.numpy as jnp
from jax import lax
from jax.experimental import pallas as pl
from jax.experimental.pallas import tpu as pltpu
from jax.sharding import PartitionSpec as P

BLOCKS = 8
BATCH = 4
NT = (((1,), (1,)), ((), ()))
NN = (((1,), (0,)), ((), ()))
F32 = jnp.float32
BF16 = jnp.bfloat16
MESH = pl.DeviceIdType.MESH


def split(x):
    high = x.astype(BF16)
    return high, (x - high.astype(F32)).astype(BF16)


def dot(left, right, dims):
    return lax.dot_general(left, right, dims, preferred_element_type=F32)


def kernel(
    nper,
    nreg,
    trans_hbm,
    force_hbm,
    term_hbm,
    part_hbm,
    share_hbm,
    costate,
    traded,
    mixer,
    maps,
    force,
    term,
    part,
    share,
    offsets,
    unit,
    outgoing,
    incoming,
    shifts,
    given,
    edges,
    starts,
    flow,
    load_sem,
    small_sem,
    map_send,
    map_recv,
    shift_send,
    shift_recv,
    edge_send,
    edge_recv,
    flow_send,
    flow_recv,
):
    rows, per, sec = force.shape
    here, zone = lax.axis_index("period"), lax.axis_index("region")
    batches = rows // BATCH
    chunk = per // 4
    share_t = per // nreg
    half = rows // 2

    barrier = pltpu.get_barrier_semaphore()
    for step in range(1, nper):
        pl.semaphore_signal(
            barrier, inc=1, device_id=(lax.rem(here + step, nper), zone), device_id_type=MESH
        )
    for step in range(1, nreg):
        pl.semaphore_signal(
            barrier, inc=1, device_id=(here, lax.rem(zone + step, nreg)), device_id_type=MESH
        )

    def row_of(k, i):
        skew = k + lax.div(k, 2) * (1 - 2 * lax.rem(k, 2))
        along_x = lax.rem(lax.div(here, BATCH) + i, batches)
        return along_x * BATCH + lax.rem(here + i + skew, BATCH)

    def slot_of(row):
        i = lax.rem(lax.div(row, BATCH) + batches - lax.div(here, BATCH), batches)
        skew = lax.rem(row + 2 * BATCH - lax.rem(here, BATCH) - i, BATCH)
        k = skew + lax.div(skew, 2) * (1 - 2 * lax.rem(skew, 2))
        return k * BATCH + i

    def load(k, c, i):
        when = pl.ds(per - chunk * (c + 1), chunk)
        return pltpu.make_async_copy(
            trans_hbm.at[row_of(k, i), when], maps.at[k * BATCH + i, when], load_sem.at[k, c, i]
        )

    small = [
        pltpu.make_async_copy(src, dst, small_sem.at[i])
        for i, (src, dst) in enumerate(
            [(force_hbm, force), (term_hbm, term), (part_hbm, part), (share_hbm, share)]
        )
    ]
    small[0].start()
    for c in range(4):
        for i in range(BATCH):
            load(0, c, i).start()
    for copy in small[1:]:
        copy.start()

    square = (sec, sec)
    eye = lax.broadcasted_iota(jnp.int32, square, 0) == lax.broadcasted_iota(jnp.int32, square, 1)
    unit[...] = jnp.where(eye, 1.0, 0.0)
    top = lax.broadcasted_iota(jnp.int32, (16, sec), 0) == 0

    def move_map(slot, source, target):
        return [
            pltpu.make_async_remote_copy(
                src_ref=src.at[slot],
                dst_ref=dst.at[source],
                send_sem=send.at[slot],
                recv_sem=recv.at[source],
                device_id=(target, zone),
                device_id_type=MESH,
            )
            for src, dst, send, recv in [
                (outgoing, incoming, map_send, map_recv),
                (shifts, given, shift_send, shift_recv),
            ]
        ]

    def send_map(k, i):
        return move_map(k * BATCH + i, here, row_of(k, i))

    def keep_map():
        return [
            pltpu.make_async_copy(outgoing.at[0], incoming.at[here], map_recv.at[here]),
            pltpu.make_async_copy(shifts.at[0], given.at[here], shift_recv.at[here]),
        ]

    small[0].wait()

    def compose(k, carry):
        @pl.when(k < batches - 1)
        def _():
            for c in range(4):
                for i in range(BATCH):
                    load(k + 1, c, i).start()

        for c in range(4):
            for i in range(BATCH):
                load(k, c, i).wait()
            for inner in range(chunk):
                t = per - 1 - chunk * c - inner
                for i in range(BATCH):
                    row, slot = row_of(k, i), k * BATCH + i
                    block = maps[slot, t]
                    source = force[row, t : t + 1]
                    if t == per - 1:
                        prod = block.T
                        offset = jnp.broadcast_to(source, (8, sec))
                    else:
                        high, low = split(block - unit[...])
                        late, late_offset = maps[slot, t + 1], offsets[slot, t + 1 : t + 2]
                        late_high, late_low = split(late)
                        tail_high, tail_low = split(jnp.where(top, late_offset, 0.0))
                        tall_high = jnp.concatenate([late_high, tail_high], 0)
                        tall_low = jnp.concatenate([late_low, tail_low], 0)
                        prod = dot(
                            jnp.concatenate([tall_high, tall_low, tall_high], 1),
                            jnp.concatenate([high, high, low], 1),
                            NT,
                        )
                        offset = prod[sec : sec + 8] + late_offset + source
                        prod = prod[:sec] + late
                    maps[slot, t] = prod
                    offsets[slot, t : t + 1] = offset[:1]
                    if t == 0:
                        outgoing[slot] = prod
                        shifts[slot] = offset[:1]

        @pl.when(k == 0)
        def _():
            pl.semaphore_wait(barrier, nper + nreg - 2)

        for i in (2, 1, 3, 0):
            row = row_of(k, i)

            @pl.when((row != here) & (here != 0))
            def _(i=i):
                for copy in send_map(k, i):
                    copy.start()

            @pl.when((row == here) & (here != 0))
            def _():
                for copy in keep_map():
                    copy.start()

        return carry

    lax.fori_loop(0, batches, compose, 0)

    for copy in small[1:]:
        copy.wait()

    region = lax.broadcasted_iota(jnp.int32, square, 0)
    for g in range(BLOCKS):
        ids, amounts = part[g], share[g]
        trade = jnp.zeros(square, F32)
        for j in range(ids.shape[0]):
            trade += jnp.where(ids[j : j + 1] == region, amounts[j : j + 1], 0.0)
        high, low = split(trade.T)
        side = sec * (g % 2)
        mixer[g // 2, :sec, side : side + sec] = high
        mixer[g // 2, sec:, side : side + sec] = low

    def upright(vector):
        return jnp.sum(jnp.where(eye, vector, 0.0), axis=1, keepdims=True)

    def send_edge(p):
        return pltpu.make_async_remote_copy(
            src_ref=edges.at[p],
            dst_ref=starts.at[here],
            send_sem=edge_send.at[p],
            recv_sem=edge_recv.at[here],
            device_id=(p, zone),
            device_id_type=MESH,
        )

    def keep_edge():
        return pltpu.make_async_copy(edges.at[here], starts.at[here], edge_recv.at[here])

    def ship_edge(p):
        @pl.when(p != here)
        def _():
            send_edge(p).start()

        @pl.when(p == here)
        def _():
            keep_edge().start()

    state = term[pl.ds(here, 1), :]
    edges[nper - 1] = state

    def chain(step, state):
        p = nper - 1 - step

        @pl.when(p != here)
        def _():
            for copy in move_map(p, p, p):
                copy.wait_recv()

        @pl.when(p == here)
        def _():
            for copy in keep_map():
                copy.wait()

        ship_edge(p)
        moved = incoming[p] * upright(state)
        state = jnp.sum(moved, axis=0, keepdims=True) + given[p]
        edges[p - 1] = state
        return state

    lax.fori_loop(0, nper - 1, chain, state)
    ship_edge(0)

    def finish(i, carry):
        row = lax.rem(lax.div(here, half) * half + i, rows)
        slot = slot_of(row)

        @pl.when(row != here)
        def _():
            pltpu.make_async_remote_copy(
                src_ref=edges.at[row],
                dst_ref=starts.at[row],
                send_sem=edge_send.at[row],
                recv_sem=edge_recv.at[row],
                device_id=(row, zone),
                device_id_type=MESH,
            ).wait_recv()

        @pl.when(row == here)
        def _():
            keep_edge().wait()

        column = jnp.broadcast_to(upright(starts[row]), square)
        lines = [jnp.sum(maps[slot, t] * column, axis=0, keepdims=True) for t in range(per)]
        value = jnp.concatenate(lines, 0) + offsets[slot]
        costate[row] = value
        bent = jnp.tanh(value)
        for t in range(per):
            flow[t, pl.ds(row, 1), :] = bent[t : t + 1]
        return carry

    def send_flow(other, h):
        mine = pl.multiple_of(zone * rows + h * half, 8)
        return pltpu.make_async_remote_copy(
            src_ref=flow.at[pl.ds(other * share_t, share_t), pl.ds(h * half, half)],
            dst_ref=traded.at[:, pl.ds(mine, half)],
            send_sem=flow_send.at[other, h],
            recv_sem=flow_recv.at[zone, h],
            device_id=(here, other),
            device_id_type=MESH,
        )

    def keep_flow(h):
        mine = pl.multiple_of(zone * rows + h * half, 8)
        return pltpu.make_async_copy(
            flow.at[pl.ds(zone * share_t, share_t), pl.ds(h * half, half)],
            traded.at[:, pl.ds(mine, half)],
            flow_recv.at[zone, h],
        )

    def got_flow(other, h):
        theirs = pl.multiple_of(other * rows + h * half, 8)
        return pltpu.make_async_remote_copy(
            src_ref=flow.at[pl.ds(other * share_t, share_t), pl.ds(h * half, half)],
            dst_ref=traded.at[:, pl.ds(theirs, half)],
            send_sem=flow_send.at[other, h],
            recv_sem=flow_recv.at[other, h],
            device_id=(here, other),
            device_id_type=MESH,
        )

    for part_no in range(2):
        lax.fori_loop(part_no * half, (part_no + 1) * half, finish, 0)
        h = lax.rem(lax.div(here, half) + part_no, 2)
        for step in range(1, nreg):
            send_flow(lax.rem(zone + step, nreg), h).start()
        keep_flow(h).start()

    def drain(row, carry):
        @pl.when(row != here)
        def _():
            send_edge(row).wait_send()

        @pl.when((row > 0) & (here != 0))
        def _():
            for copy in move_map(row, here, row):
                copy.wait_send()

        return carry

    lax.fori_loop(0, rows, drain, 0)

    for part_no in range(2):
        h = lax.rem(lax.div(here, half) + part_no, 2)
        for step in range(1, nreg):
            got_flow(lax.rem(zone + step, nreg), h).wait_recv()
        keep_flow(h).wait()

    for step in range(1, nreg):
        for h in range(2):
            send_flow(lax.rem(zone + step, nreg), h).wait_send()


def mix(traded, mixer, costate, costate_hbm, clear_hbm, clear, out_sem):
    share_t, sec = traded.shape[0], traded.shape[2]
    save = pltpu.make_async_copy(costate, costate_hbm, out_sem.at[0])
    save.start()
    width = share_t * sec
    whole = jnp.concatenate([traded[t] for t in range(share_t)], 1)
    high, low = split(whole)
    group = lax.div(
        lax.rem(lax.broadcasted_iota(jnp.int32, (1, width), 1), sec), sec // BLOCKS
    )
    mixed = jnp.zeros((sec, width), F32)
    for pair in range(BLOCKS // 2):
        masks = [group == 2 * pair, group == 2 * pair + 1]
        tall_high = jnp.concatenate([jnp.where(m, high, BF16(0)) for m in masks], 0)
        tall_low = jnp.concatenate([jnp.where(m, low, BF16(0)) for m in masks], 0)
        first = dot(mixer[pair], tall_high, NN)
        mixed += first[:sec] + first[sec:]
        mixed += dot(mixer[pair, :sec], tall_low, NN)
    result = whole - mixed
    for t in range(share_t):
        clear[:, t, :] = result[:, t * sec : (t + 1) * sec]
    done = pltpu.make_async_copy(clear, clear_hbm, out_sem.at[1])
    done.start()
    save.wait()
    done.wait()


def shards(nper, nreg, transition, forcing, terminal, partners, shares):
    rows, per, sec = forcing.shape
    regions = partners.shape[1]
    share_t = per // nreg
    ids, amounts = jnp.swapaxes(partners, 1, 2), jnp.swapaxes(shares, 1, 2)
    anywhere = pl.BlockSpec(memory_space=pl.ANY)
    local = pl.BlockSpec(memory_space=pltpu.VMEM)
    dma = pltpu.SemaphoreType.DMA
    costate, traded, mixer = pl.pallas_call(
        functools.partial(kernel, nper, nreg),
        out_shape=(
            pltpu.VMEM((rows, per, sec), F32),
            pltpu.VMEM((share_t, regions, sec), F32),
            pltpu.VMEM((BLOCKS // 2, 2 * regions, 2 * regions), BF16),
        ),
        in_specs=[anywhere] * 5,
        out_specs=[local] * 3,
        scratch_shapes=[
            pltpu.VMEM((rows, per, sec, sec), F32),
            pltpu.VMEM((rows, per, sec), F32),
            pltpu.VMEM((rows, sec), F32),
            pltpu.VMEM(ids.shape, jnp.int32),
            pltpu.VMEM(amounts.shape, F32),
            pltpu.VMEM((rows, per, sec), F32),
            pltpu.VMEM((sec, sec), F32),
            pltpu.VMEM((rows, sec, sec), F32),
            pltpu.VMEM((nper, sec, sec), F32),
            pltpu.VMEM((rows, 1, sec), F32),
            pltpu.VMEM((nper, 1, sec), F32),
            pltpu.VMEM((nper, 1, sec), F32),
            pltpu.VMEM((rows, 1, sec), F32),
            pltpu.VMEM((per, rows, sec), F32),
            dma((rows // BATCH, 4, BATCH)),
            dma((4,)),
            dma((rows,)),
            dma((nper,)),
            dma((rows,)),
            dma((nper,)),
            dma((nper,)),
            dma((rows,)),
            dma((nreg, 2)),
            dma((nreg, 2)),
        ],
        compiler_params=pltpu.CompilerParams(
            collective_id=0, has_side_effects=True, vmem_limit_bytes=60 * 2**20
        ),
        name="newton_step",
    )(transition, forcing, terminal, ids, amounts)
    return pl.pallas_call(
        mix,
        out_shape=(
            jax.ShapeDtypeStruct((rows, per, sec), F32),
            jax.ShapeDtypeStruct((regions, share_t, sec), F32),
        ),
        in_specs=[local] * 3,
        out_specs=[anywhere] * 2,
        scratch_shapes=[pltpu.VMEM((regions, share_t, sec), F32), dma((2,))],
        compiler_params=pltpu.CompilerParams(vmem_limit_bytes=8 * 2**20),
        name="trade_mix",
    )(traded, mixer, costate)


def solution(mesh):
    return jax.shard_map(
        functools.partial(shards, mesh.shape["period"], mesh.shape["region"]),
        mesh=mesh,
        in_specs=(
            P("region", "period", None, None),
            P("region", "period", None),
            P("region", None),
            P(),
            P(),
        ),
        out_specs=(P("region", "period", None), P(None, ("period", "region"), None)),
        check_vma=False,
    )
```

```python
import functools

import jax
import jax.numpy as jnp
from jax import lax
from jax.experimental import pallas as pl
from jax.experimental.pallas import tpu as pltpu
from jax.sharding import PartitionSpec as P

BLOCKS = 8
BATCH = 4
NT = (((1,), (1,)), ((), ()))
NN = (((1,), (0,)), ((), ()))
F32 = jnp.float32
BF16 = jnp.bfloat16
MESH = pl.DeviceIdType.MESH


def split(x):
    high = x.astype(BF16)
    return high, (x - high.astype(F32)).astype(BF16)


def dot(left, right, dims):
    return lax.dot_general(left, right, dims, preferred_element_type=F32)


def kernel(
    nper,
    nreg,
    trans_hbm,
    force_hbm,
    term_hbm,
    part_hbm,
    share_hbm,
    costate,
    traded,
    mixer,
    maps,
    force,
    term,
    part,
    share,
    offsets,
    unit,
    outgoing,
    incoming,
    shifts,
    given,
    edges,
    starts,
    columns,
    flow,
    load_sem,
    small_sem,
    map_send,
    map_recv,
    shift_send,
    shift_recv,
    edge_send,
    edge_recv,
    flow_send,
    flow_recv,
):
    rows, per, sec = force.shape
    here, zone = lax.axis_index("period"), lax.axis_index("region")
    batches = rows // BATCH
    chunk = per // 4
    share_t = per // nreg

    barrier = pltpu.get_barrier_semaphore()
    for step in range(1, nper):
        pl.semaphore_signal(
            barrier, inc=1, device_id=(lax.rem(here + step, nper), zone), device_id_type=MESH
        )
    for step in range(1, nreg):
        pl.semaphore_signal(
            barrier, inc=1, device_id=(here, lax.rem(zone + step, nreg)), device_id_type=MESH
        )

    def row_of(k, i):
        skew = k + lax.div(k, 2) * (1 - 2 * lax.rem(k, 2))
        along_x = lax.rem(lax.div(here, BATCH) + i, batches)
        return along_x * BATCH + lax.rem(here + i + skew, BATCH)

    def load(k, c, i):
        when = pl.ds(per - chunk * (c + 1), chunk)
        return pltpu.make_async_copy(
            trans_hbm.at[row_of(k, i), when], maps.at[k * BATCH + i, when], load_sem.at[k, c, i]
        )

    small = [
        pltpu.make_async_copy(src, dst, small_sem.at[i])
        for i, (src, dst) in enumerate(
            [(force_hbm, force), (term_hbm, term), (part_hbm, part), (share_hbm, share)]
        )
    ]
    small[0].start()
    for c in range(4):
        for i in range(BATCH):
            load(0, c, i).start()
    for copy in small[1:]:
        copy.start()

    square = (sec, sec)
    eye = lax.broadcasted_iota(jnp.int32, square, 0) == lax.broadcasted_iota(jnp.int32, square, 1)
    unit[...] = jnp.where(eye, 1.0, 0.0)
    top = lax.broadcasted_iota(jnp.int32, (16, sec), 0) == 0

    def move_map(slot, source, target):
        return [
            pltpu.make_async_remote_copy(
                src_ref=src.at[slot],
                dst_ref=dst.at[source],
                send_sem=send.at[slot],
                recv_sem=recv.at[source],
                device_id=(target, zone),
                device_id_type=MESH,
            )
            for src, dst, send, recv in [
                (outgoing, incoming, map_send, map_recv),
                (shifts, given, shift_send, shift_recv),
            ]
        ]

    def send_map(k, i):
        return move_map(k * BATCH + i, here, row_of(k, i))

    def keep_map():
        return [
            pltpu.make_async_copy(outgoing.at[0], incoming.at[here], map_recv.at[here]),
            pltpu.make_async_copy(shifts.at[0], given.at[here], shift_recv.at[here]),
        ]

    small[0].wait()

    def compose(k, carry):
        @pl.when(k < batches - 1)
        def _():
            for c in range(4):
                for i in range(BATCH):
                    load(k + 1, c, i).start()

        for c in range(4):
            for i in range(BATCH):
                load(k, c, i).wait()
            for inner in range(chunk):
                t = per - 1 - chunk * c - inner
                for i in range(BATCH):
                    row, slot = row_of(k, i), k * BATCH + i
                    block = maps[slot, t]
                    source = force[row, t : t + 1]
                    if t == per - 1:
                        prod = block.T
                        offset = jnp.broadcast_to(source, (8, sec))
                    else:
                        high, low = split(block - unit[...])
                        late, late_offset = maps[slot, t + 1], offsets[slot, t + 1 : t + 2]
                        late_high, late_low = split(late)
                        tail_high, tail_low = split(jnp.where(top, late_offset, 0.0))
                        tall_high = jnp.concatenate([late_high, tail_high], 0)
                        tall_low = jnp.concatenate([late_low, tail_low], 0)
                        prod = dot(
                            jnp.concatenate([tall_high, tall_low, tall_high], 1),
                            jnp.concatenate([high, high, low], 1),
                            NT,
                        )
                        offset = prod[sec : sec + 8] + late_offset + source
                        prod = prod[:sec] + late
                    maps[slot, t] = prod
                    offsets[slot, t : t + 1] = offset[:1]
                    if t == 0:
                        outgoing[slot] = prod
                        shifts[slot] = offset[:1]

        @pl.when(k == 0)
        def _():
            pl.semaphore_wait(barrier, nper + nreg - 2)

        for i in (2, 1, 3, 0):
            row = row_of(k, i)

            @pl.when((row != here) & (here != 0))
            def _(i=i):
                for copy in send_map(k, i):
                    copy.start()

            @pl.when((row == here) & (here != 0))
            def _():
                for copy in keep_map():
                    copy.start()

        return carry

    lax.fori_loop(0, batches, compose, 0)

    for copy in small[1:]:
        copy.wait()

    region = lax.broadcasted_iota(jnp.int32, square, 0)
    for g in range(BLOCKS):
        ids, amounts = part[g], share[g]
        trade = jnp.zeros(square, F32)
        for j in range(ids.shape[0]):
            trade += jnp.where(ids[j : j + 1] == region, amounts[j : j + 1], 0.0)
        high, low = split(trade.T)
        side = sec * (g % 2)
        mixer[g // 2, :sec, side : side + sec] = high
        mixer[g // 2, sec:, side : side + sec] = low

    def upright(vector):
        return jnp.sum(jnp.where(eye, vector, 0.0), axis=1, keepdims=True)

    def send_edge(p):
        return pltpu.make_async_remote_copy(
            src_ref=edges.at[p],
            dst_ref=starts.at[here],
            send_sem=edge_send.at[p],
            recv_sem=edge_recv.at[here],
            device_id=(p, zone),
            device_id_type=MESH,
        )

    def keep_edge():
        return pltpu.make_async_copy(edges.at[here], starts.at[here], edge_recv.at[here])

    def ship_edge(p):
        @pl.when(p != here)
        def _():
            send_edge(p).start()

        @pl.when(p == here)
        def _():
            keep_edge().start()

    state = term[pl.ds(here, 1), :]
    edges[nper - 1] = state

    def chain(step, state):
        p = nper - 1 - step

        @pl.when(p != here)
        def _():
            for copy in move_map(p, p, p):
                copy.wait_recv()

        @pl.when(p == here)
        def _():
            for copy in keep_map():
                copy.wait()

        ship_edge(p)
        moved = incoming[p] * upright(state)
        state = jnp.sum(moved, axis=0, keepdims=True) + given[p]
        edges[p - 1] = state
        return state

    lax.fori_loop(0, nper - 1, chain, state)
    ship_edge(0)

    def arrive(k, carry):
        for i in range(BATCH):
            row = row_of(k, i)

            @pl.when(row != here)
            def _(row=row):
                pltpu.make_async_remote_copy(
                    src_ref=edges.at[row],
                    dst_ref=starts.at[row],
                    send_sem=edge_send.at[row],
                    recv_sem=edge_recv.at[row],
                    device_id=(row, zone),
                    device_id_type=MESH,
                ).wait_recv()

            @pl.when(row == here)
            def _():
                keep_edge().wait()

        for i in range(BATCH):
            column = upright(starts[row_of(k, i)])
            columns[k * BATCH + i] = jnp.broadcast_to(column, square)
        return carry

    lax.fori_loop(0, batches, arrive, 0)

    def send_flow(other):
        return pltpu.make_async_remote_copy(
            src_ref=flow.at[pl.ds(other * share_t, share_t)],
            dst_ref=traded.at[:, pl.ds(pl.multiple_of(zone * rows, 8), rows)],
            send_sem=flow_send.at[other],
            recv_sem=flow_recv.at[zone],
            device_id=(here, other),
            device_id_type=MESH,
        )

    def keep_flow():
        return pltpu.make_async_copy(
            flow.at[pl.ds(zone * share_t, share_t)],
            traded.at[:, pl.ds(pl.multiple_of(zone * rows, 8), rows)],
            flow_recv.at[zone],
        )

    def got_flow(other):
        return pltpu.make_async_remote_copy(
            src_ref=flow.at[pl.ds(other * share_t, share_t)],
            dst_ref=traded.at[:, pl.ds(pl.multiple_of(other * rows, 8), rows)],
            send_sem=flow_send.at[other],
            recv_sem=flow_recv.at[other],
            device_id=(here, other),
            device_id_type=MESH,
        )

    layers = nreg // 2
    order = [(dz, dc) for dz in (2, 1, 3, 0) if dz < layers for dc in (1, 0)]
    others = []
    for dz, dc in order:
        other = lax.rem(lax.div(zone, 2) + dz, layers) * 2 + lax.rem(zone + dc, 2)
        for step in range(share_t):
            t = other * share_t + step
            for k in range(batches):
                for i in range(BATCH):
                    slot, row = k * BATCH + i, row_of(k, i)
                    value = jnp.sum(maps[slot, t] * columns[slot], axis=0, keepdims=True)
                    value += offsets[slot, pl.ds(t, 1), :]
                    costate[row, pl.ds(t, 1), :] = value
                    flow[t, pl.ds(row, 1), :] = value
            flow[t] = jnp.tanh(flow[t])
        if (dz, dc) != (0, 0):
            others.append(other)
            send_flow(other).start()
        else:
            keep_flow().start()

    def drain(row, carry):
        @pl.when(row != here)
        def _():
            send_edge(row).wait_send()

        @pl.when((row > 0) & (here != 0))
        def _():
            for copy in move_map(row, here, row):
                copy.wait_send()

        return carry

    lax.fori_loop(0, rows, drain, 0)

    keep_flow().wait()
    for other in others:
        got_flow(other).wait_recv()
    for other in others:
        send_flow(other).wait_send()


def mix(traded, mixer, costate, costate_hbm, clear_hbm, clear, out_sem):
    share_t, sec = traded.shape[0], traded.shape[2]
    save = pltpu.make_async_copy(costate, costate_hbm, out_sem.at[0])
    save.start()
    width = share_t * sec
    whole = jnp.concatenate([traded[t] for t in range(share_t)], 1)
    high, low = split(whole)
    group = lax.div(
        lax.rem(lax.broadcasted_iota(jnp.int32, (1, width), 1), sec), sec // BLOCKS
    )
    mixed = jnp.zeros((sec, width), F32)
    for pair in range(BLOCKS // 2):
        masks = [group == 2 * pair, group == 2 * pair + 1]
        tall_high = jnp.concatenate([jnp.where(m, high, BF16(0)) for m in masks], 0)
        tall_low = jnp.concatenate([jnp.where(m, low, BF16(0)) for m in masks], 0)
        first = dot(mixer[pair], tall_high, NN)
        mixed += first[:sec] + first[sec:]
        mixed += dot(mixer[pair, :sec], tall_low, NN)
    result = whole - mixed
    for t in range(share_t):
        clear[:, t, :] = result[:, t * sec : (t + 1) * sec]
    done = pltpu.make_async_copy(clear, clear_hbm, out_sem.at[1])
    done.start()
    save.wait()
    done.wait()


def shards(nper, nreg, transition, forcing, terminal, partners, shares):
    rows, per, sec = forcing.shape
    regions = partners.shape[1]
    share_t = per // nreg
    ids, amounts = jnp.swapaxes(partners, 1, 2), jnp.swapaxes(shares, 1, 2)
    anywhere = pl.BlockSpec(memory_space=pl.ANY)
    local = pl.BlockSpec(memory_space=pltpu.VMEM)
    dma = pltpu.SemaphoreType.DMA
    costate, traded, mixer = pl.pallas_call(
        functools.partial(kernel, nper, nreg),
        out_shape=(
            pltpu.VMEM((rows, per, sec), F32),
            pltpu.VMEM((share_t, regions, sec), F32),
            pltpu.VMEM((BLOCKS // 2, 2 * regions, 2 * regions), BF16),
        ),
        in_specs=[anywhere] * 5,
        out_specs=[local] * 3,
        scratch_shapes=[
            pltpu.VMEM((rows, per, sec, sec), F32),
            pltpu.VMEM((rows, per, sec), F32),
            pltpu.VMEM((rows, sec), F32),
            pltpu.VMEM(ids.shape, jnp.int32),
            pltpu.VMEM(amounts.shape, F32),
            pltpu.VMEM((rows, per, sec), F32),
            pltpu.VMEM((sec, sec), F32),
            pltpu.VMEM((rows, sec, sec), F32),
            pltpu.VMEM((nper, sec, sec), F32),
            pltpu.VMEM((rows, 1, sec), F32),
            pltpu.VMEM((nper, 1, sec), F32),
            pltpu.VMEM((nper, 1, sec), F32),
            pltpu.VMEM((rows, 1, sec), F32),
            pltpu.VMEM((rows, sec, sec), F32),
            pltpu.VMEM((per, rows, sec), F32),
            dma((rows // BATCH, 4, BATCH)),
            dma((4,)),
            dma((rows,)),
            dma((nper,)),
            dma((rows,)),
            dma((nper,)),
            dma((nper,)),
            dma((rows,)),
            dma((nreg,)),
            dma((nreg,)),
        ],
        compiler_params=pltpu.CompilerParams(
            collective_id=0, has_side_effects=True, vmem_limit_bytes=60 * 2**20
        ),
        name="newton_step",
    )(transition, forcing, terminal, ids, amounts)
    return pl.pallas_call(
        mix,
        out_shape=(
            jax.ShapeDtypeStruct((rows, per, sec), F32),
            jax.ShapeDtypeStruct((regions, share_t, sec), F32),
        ),
        in_specs=[local] * 3,
        out_specs=[anywhere] * 2,
        scratch_shapes=[pltpu.VMEM((regions, share_t, sec), F32), dma((2,))],
        compiler_params=pltpu.CompilerParams(vmem_limit_bytes=8 * 2**20),
        name="trade_mix",
    )(traded, mixer, costate)


def solution(mesh):
    return jax.shard_map(
        functools.partial(shards, mesh.shape["period"], mesh.shape["region"]),
        mesh=mesh,
        in_specs=(
            P("region", "period", None, None),
            P("region", "period", None),
            P("region", None),
            P(),
            P(),
        ),
        out_specs=(P("region", "period", None), P(None, ("period", "region"), None)),
        check_vma=False,
    )
```

```python
import functools

import jax
import jax.numpy as jnp
from jax import lax
from jax.experimental import pallas as pl
from jax.experimental.pallas import tpu as pltpu
from jax.sharding import PartitionSpec as P

BLOCKS = 8
BATCH = 4
NT = (((1,), (1,)), ((), ()))
NN = (((1,), (0,)), ((), ()))
F32 = jnp.float32
BF16 = jnp.bfloat16
MESH = pl.DeviceIdType.MESH


def split(x):
    high = x.astype(BF16)
    return high, (x - high.astype(F32)).astype(BF16)


def dot(left, right, dims):
    return lax.dot_general(left, right, dims, preferred_element_type=F32)


def kernel(
    nper,
    nreg,
    trans_hbm,
    force_hbm,
    term_hbm,
    part_hbm,
    share_hbm,
    costate,
    traded,
    mixer,
    maps,
    force,
    term,
    part,
    share,
    offsets,
    unit,
    outgoing,
    incoming,
    shifts,
    given,
    edges,
    starts,
    columns,
    flow,
    load_sem,
    small_sem,
    map_send,
    map_recv,
    shift_send,
    shift_recv,
    edge_send,
    edge_recv,
    flow_send,
    flow_recv,
):
    rows, per, sec = force.shape
    here, zone = lax.axis_index("period"), lax.axis_index("region")
    batches = rows // BATCH
    chunk = per // 4
    share_t = per // nreg

    barrier = pltpu.get_barrier_semaphore()
    for step in range(1, nper):
        pl.semaphore_signal(
            barrier, inc=1, device_id=(lax.rem(here + step, nper), zone), device_id_type=MESH
        )
    for step in range(1, nreg):
        pl.semaphore_signal(
            barrier, inc=1, device_id=(here, lax.rem(zone + step, nreg)), device_id_type=MESH
        )

    swapped = lax.rem(zone, 2) == 1
    at_x, at_y = lax.div(here, BATCH), lax.rem(here, BATCH)
    last = nper - 1

    def row_of(k, i):
        skew = k + lax.div(k, 2) * (1 - 2 * lax.rem(k, 2))
        other = lax.rem(i + skew, BATCH)
        along_x, along_y = jnp.where(swapped, other, i), jnp.where(swapped, i, other)
        return lax.rem(at_x + along_x, batches) * BATCH + lax.rem(at_y + along_y, BATCH)

    def load(k, c, i):
        when = pl.ds(per - chunk * (c + 1), chunk)
        return pltpu.make_async_copy(
            trans_hbm.at[row_of(k, i), when], maps.at[k * BATCH + i, when], load_sem.at[k, c, i]
        )

    small = [
        pltpu.make_async_copy(src, dst, small_sem.at[i])
        for i, (src, dst) in enumerate(
            [(force_hbm, force), (term_hbm, term), (part_hbm, part), (share_hbm, share)]
        )
    ]
    for copy in small:
        copy.start()
    for c in range(4):
        for i in range(BATCH):
            load(0, c, i).start()

    square = (sec, sec)
    eye = lax.broadcasted_iota(jnp.int32, square, 0) == lax.broadcasted_iota(jnp.int32, square, 1)
    unit[...] = jnp.where(eye, 1.0, 0.0)
    top = lax.broadcasted_iota(jnp.int32, (16, sec), 0) == 0

    def upright(vector):
        return jnp.sum(jnp.where(eye, vector, 0.0), axis=1, keepdims=True)

    def move_map(slot, source, target):
        return [
            pltpu.make_async_remote_copy(
                src_ref=src.at[slot],
                dst_ref=dst.at[source],
                send_sem=send.at[slot],
                recv_sem=recv.at[source],
                device_id=(target, zone),
                device_id_type=MESH,
            )
            for src, dst, send, recv in [
                (outgoing, incoming, map_send, map_recv),
                (shifts, given, shift_send, shift_recv),
            ]
        ]

    def send_map(k, i):
        return move_map(k * BATCH + i, here, row_of(k, i))

    def keep_map():
        return [
            pltpu.make_async_copy(outgoing.at[0], incoming.at[here], map_recv.at[here]),
            pltpu.make_async_copy(shifts.at[0], given.at[here], shift_recv.at[here]),
        ]

    for copy in small[:2]:
        copy.wait()

    def compose(k, carry):
        @pl.when(k < batches - 1)
        def _():
            for c in range(4):
                for i in range(BATCH):
                    load(k + 1, c, i).start()

        for c in range(4):
            for i in range(BATCH):
                load(k, c, i).wait()
            for inner in range(chunk):
                t = per - 1 - chunk * c - inner
                for i in range(BATCH):
                    row, slot = row_of(k, i), k * BATCH + i
                    block = maps[slot, t]
                    source = force[row, t : t + 1]
                    if t == per - 1:
                        prod = block.T
                        offset = jnp.broadcast_to(source, (8, sec))
                    else:
                        high, low = split(block - unit[...])
                        late, late_offset = maps[slot, t + 1], offsets[slot, t + 1 : t + 2]
                        late_high, late_low = split(late)
                        tail_high, tail_low = split(jnp.where(top, late_offset, 0.0))
                        tall_high = jnp.concatenate([late_high, tail_high], 0)
                        tall_low = jnp.concatenate([late_low, tail_low], 0)
                        prod = dot(
                            jnp.concatenate([tall_high, tall_low, tall_high], 1),
                            jnp.concatenate([high, high, low], 1),
                            NT,
                        )
                        offset = prod[sec : sec + 8] + late_offset + source
                        prod = prod[:sec] + late
                    maps[slot, t] = prod
                    offsets[slot, t : t + 1] = offset[:1]
                    if t == 0:
                        outgoing[slot] = prod
                        shifts[slot] = offset[:1]

        @pl.when(k == 0)
        def _():
            pl.semaphore_wait(barrier, nper + nreg - 2)

        @pl.when(here == last)
        def _():
            for i in range(BATCH):
                slot = k * BATCH + i
                column = upright(term[pl.ds(row_of(k, i), 1), :])
                value = jnp.sum(maps[slot, 0] * column, axis=0, keepdims=True)
                shifts[slot] = value + offsets[slot, 0:1]

        for i in (2, 1, 3, 0):
            row = row_of(k, i)

            @pl.when((row != here) & (here != 0))
            def _(i=i):
                send_map(k, i)[1].start()

            @pl.when((row != here) & (here != 0) & (here != last))
            def _(i=i):
                send_map(k, i)[0].start()

            @pl.when((row == here) & (here != 0))
            def _():
                keep_map()[1].start()

            @pl.when((row == here) & (here != 0) & (here != last))
            def _():
                keep_map()[0].start()

        return carry

    lax.fori_loop(0, batches, compose, 0)

    for copy in small[2:]:
        copy.wait()

    region = lax.broadcasted_iota(jnp.int32, square, 0)
    for g in range(BLOCKS):
        ids, amounts = part[g], share[g]
        trade = jnp.zeros(square, F32)
        for j in range(ids.shape[0]):
            trade += jnp.where(ids[j : j + 1] == region, amounts[j : j + 1], 0.0)
        high, low = split(trade.T)
        side = sec * (g % 2)
        mixer[g // 2, :sec, side : side + sec] = high
        mixer[g // 2, sec:, side : side + sec] = low

    def send_edge(p):
        return pltpu.make_async_remote_copy(
            src_ref=edges.at[p],
            dst_ref=starts.at[here],
            send_sem=edge_send.at[p],
            recv_sem=edge_recv.at[here],
            device_id=(p, zone),
            device_id_type=MESH,
        )

    def keep_edge():
        return pltpu.make_async_copy(edges.at[here], starts.at[here], edge_recv.at[here])

    def ship_edge(p):
        @pl.when(p != here)
        def _():
            send_edge(p).start()

        @pl.when(p == here)
        def _():
            keep_edge().start()

    edges[last] = term[pl.ds(here, 1), :]
    ship_edge(last)

    @pl.when(here != last)
    def _():
        move_map(last, last, last)[1].wait_recv()

    @pl.when(here == last)
    def _():
        keep_map()[1].wait()

    state = given[last]
    edges[last - 1] = state

    def chain(step, state):
        p = last - 1 - step

        @pl.when(p != here)
        def _():
            for copy in move_map(p, p, p):
                copy.wait_recv()

        @pl.when(p == here)
        def _():
            for copy in keep_map():
                copy.wait()

        ship_edge(p)
        moved = incoming[p] * upright(state)
        state = jnp.sum(moved, axis=0, keepdims=True) + given[p]
        edges[p - 1] = state
        return state

    lax.fori_loop(0, nper - 2, chain, state)
    ship_edge(0)

    def arrive(row, carry):
        @pl.when(row != here)
        def _():
            pltpu.make_async_remote_copy(
                src_ref=edges.at[row],
                dst_ref=starts.at[row],
                send_sem=edge_send.at[row],
                recv_sem=edge_recv.at[row],
                device_id=(row, zone),
                device_id_type=MESH,
            ).wait_recv()

        @pl.when(row == here)
        def _():
            keep_edge().wait()

        return carry

    lax.fori_loop(0, rows, arrive, 0)
    for k in range(batches):
        for i in range(BATCH):
            column = upright(starts[row_of(k, i)])
            columns[k * BATCH + i] = jnp.broadcast_to(column, square)

    def send_flow(other):
        return pltpu.make_async_remote_copy(
            src_ref=flow.at[pl.ds(other * share_t, share_t)],
            dst_ref=traded.at[:, pl.ds(pl.multiple_of(zone * rows, 8), rows)],
            send_sem=flow_send.at[other],
            recv_sem=flow_recv.at[zone],
            device_id=(here, other),
            device_id_type=MESH,
        )

    def keep_flow():
        return pltpu.make_async_copy(
            flow.at[pl.ds(zone * share_t, share_t)],
            traded.at[:, pl.ds(pl.multiple_of(zone * rows, 8), rows)],
            flow_recv.at[zone],
        )

    def got_flow(other):
        return pltpu.make_async_remote_copy(
            src_ref=flow.at[pl.ds(other * share_t, share_t)],
            dst_ref=traded.at[:, pl.ds(pl.multiple_of(other * rows, 8), rows)],
            send_sem=flow_send.at[other],
            recv_sem=flow_recv.at[other],
            device_id=(here, other),
            device_id_type=MESH,
        )

    layers = nreg // 2
    order = [(dz, dc) for dz in (2, 1, 3, 0) if dz < layers for dc in (1, 0)]
    others = []
    for dz, dc in order:
        other = lax.rem(lax.div(zone, 2) + dz, layers) * 2 + lax.rem(zone + dc, 2)
        for step in range(share_t):
            t = other * share_t + step
            for k in range(batches):
                for i in range(BATCH):
                    slot, row = k * BATCH + i, row_of(k, i)
                    value = jnp.sum(maps[slot, t] * columns[slot], axis=0, keepdims=True)
                    value += offsets[slot, pl.ds(t, 1), :]
                    costate[row, pl.ds(t, 1), :] = value
                    flow[t, pl.ds(row, 1), :] = value
            flow[t] = jnp.tanh(flow[t])
        if (dz, dc) != (0, 0):
            others.append(other)
            send_flow(other).start()
        else:
            keep_flow().start()

    def drain(row, carry):
        @pl.when(row != here)
        def _():
            send_edge(row).wait_send()

        @pl.when((row > 0) & (here != 0))
        def _():
            move_map(row, here, row)[1].wait_send()

        @pl.when((row > 0) & (here != 0) & (here != last))
        def _():
            move_map(row, here, row)[0].wait_send()

        return carry

    lax.fori_loop(0, rows, drain, 0)

    keep_flow().wait()
    for other in others:
        got_flow(other).wait_recv()
    for other in others:
        send_flow(other).wait_send()


def mix(traded, mixer, costate, costate_hbm, clear_hbm, clear, out_sem):
    share_t, sec = traded.shape[0], traded.shape[2]
    save = pltpu.make_async_copy(costate, costate_hbm, out_sem.at[0])
    save.start()
    width = share_t * sec
    whole = jnp.concatenate([traded[t] for t in range(share_t)], 1)
    high, low = split(whole)
    group = lax.div(
        lax.rem(lax.broadcasted_iota(jnp.int32, (1, width), 1), sec), sec // BLOCKS
    )
    mixed = jnp.zeros((sec, width), F32)
    for pair in range(BLOCKS // 2):
        masks = [group == 2 * pair, group == 2 * pair + 1]
        tall_high = jnp.concatenate([jnp.where(m, high, BF16(0)) for m in masks], 0)
        tall_low = jnp.concatenate([jnp.where(m, low, BF16(0)) for m in masks], 0)
        first = dot(mixer[pair], tall_high, NN)
        mixed += first[:sec] + first[sec:]
        mixed += dot(mixer[pair, :sec], tall_low, NN)
    result = whole - mixed
    for t in range(share_t):
        clear[:, t, :] = result[:, t * sec : (t + 1) * sec]
    done = pltpu.make_async_copy(clear, clear_hbm, out_sem.at[1])
    done.start()
    save.wait()
    done.wait()


def shards(nper, nreg, transition, forcing, terminal, partners, shares):
    rows, per, sec = forcing.shape
    regions = partners.shape[1]
    share_t = per // nreg
    ids, amounts = jnp.swapaxes(partners, 1, 2), jnp.swapaxes(shares, 1, 2)
    anywhere = pl.BlockSpec(memory_space=pl.ANY)
    local = pl.BlockSpec(memory_space=pltpu.VMEM)
    dma = pltpu.SemaphoreType.DMA
    costate, traded, mixer = pl.pallas_call(
        functools.partial(kernel, nper, nreg),
        out_shape=(
            pltpu.VMEM((rows, per, sec), F32),
            pltpu.VMEM((share_t, regions, sec), F32),
            pltpu.VMEM((BLOCKS // 2, 2 * regions, 2 * regions), BF16),
        ),
        in_specs=[anywhere] * 5,
        out_specs=[local] * 3,
        scratch_shapes=[
            pltpu.VMEM((rows, per, sec, sec), F32),
            pltpu.VMEM((rows, per, sec), F32),
            pltpu.VMEM((rows, sec), F32),
            pltpu.VMEM(ids.shape, jnp.int32),
            pltpu.VMEM(amounts.shape, F32),
            pltpu.VMEM((rows, per, sec), F32),
            pltpu.VMEM((sec, sec), F32),
            pltpu.VMEM((rows, sec, sec), F32),
            pltpu.VMEM((nper, sec, sec), F32),
            pltpu.VMEM((rows, 1, sec), F32),
            pltpu.VMEM((nper, 1, sec), F32),
            pltpu.VMEM((nper, 1, sec), F32),
            pltpu.VMEM((rows, 1, sec), F32),
            pltpu.VMEM((rows, sec, sec), F32),
            pltpu.VMEM((per, rows, sec), F32),
            dma((rows // BATCH, 4, BATCH)),
            dma((4,)),
            dma((rows,)),
            dma((nper,)),
            dma((rows,)),
            dma((nper,)),
            dma((nper,)),
            dma((rows,)),
            dma((nreg,)),
            dma((nreg,)),
        ],
        compiler_params=pltpu.CompilerParams(
            collective_id=0, has_side_effects=True, vmem_limit_bytes=60 * 2**20
        ),
        name="newton_step",
    )(transition, forcing, terminal, ids, amounts)
    return pl.pallas_call(
        mix,
        out_shape=(
            jax.ShapeDtypeStruct((rows, per, sec), F32),
            jax.ShapeDtypeStruct((regions, share_t, sec), F32),
        ),
        in_specs=[local] * 3,
        out_specs=[anywhere] * 2,
        scratch_shapes=[pltpu.VMEM((regions, share_t, sec), F32), dma((2,))],
        compiler_params=pltpu.CompilerParams(vmem_limit_bytes=8 * 2**20),
        name="trade_mix",
    )(traded, mixer, costate)


def solution(mesh):
    return jax.shard_map(
        functools.partial(shards, mesh.shape["period"], mesh.shape["region"]),
        mesh=mesh,
        in_specs=(
            P("region", "period", None, None),
            P("region", "period", None),
            P("region", None),
            P(),
            P(),
        ),
        out_specs=(P("region", "period", None), P(None, ("period", "region"), None)),
        check_vma=False,
    )
```

```python
import functools

import jax
import jax.numpy as jnp
from jax import lax
from jax.experimental import pallas as pl
from jax.experimental.pallas import tpu as pltpu
from jax.sharding import PartitionSpec as P

BLOCKS = 8
BATCH = 4
STEPS = (
    ((2, 2), (2, 1), (1, 2), (2, 3))
    + ((3, 2), (2, 0), (0, 2), (1, 1))
    + ((3, 3), (1, 3), (3, 1), (0, 0))
    + ((1, 0), (0, 1), (3, 0), (0, 3))
)
NT = (((1,), (1,)), ((), ()))
NN = (((1,), (0,)), ((), ()))
F32 = jnp.float32
BF16 = jnp.bfloat16
MESH = pl.DeviceIdType.MESH


def split(x):
    high = x.astype(BF16)
    return high, (x - high.astype(F32)).astype(BF16)


def dot(left, right, dims):
    return lax.dot_general(left, right, dims, preferred_element_type=F32)


def kernel(
    nper,
    nreg,
    trans_hbm,
    force_hbm,
    term_hbm,
    part_hbm,
    share_hbm,
    costate,
    traded,
    mixer,
    maps,
    force,
    term,
    part,
    share,
    offsets,
    unit,
    outgoing,
    incoming,
    shifts,
    given,
    edges,
    starts,
    columns,
    flow,
    load_sem,
    small_sem,
    map_send,
    map_recv,
    shift_send,
    shift_recv,
    edge_send,
    edge_recv,
    flow_send,
    flow_recv,
):
    rows, per, sec = force.shape
    here, zone = lax.axis_index("period"), lax.axis_index("region")
    batches = rows // BATCH
    chunk = per // 4
    share_t = per // nreg

    barrier = pltpu.get_barrier_semaphore()
    for step in range(1, nper):
        pl.semaphore_signal(
            barrier, inc=1, device_id=(lax.rem(here + step, nper), zone), device_id_type=MESH
        )
    for step in range(1, nreg):
        pl.semaphore_signal(
            barrier, inc=1, device_id=(here, lax.rem(zone + step, nreg)), device_id_type=MESH
        )

    def pick(k, table):
        found = table[-1]
        for n, entry in enumerate(table[:-1]):
            found = jnp.where(k == n, entry, found)
        return found

    at_x, at_y = lax.div(here, BATCH), lax.rem(here, BATCH)
    own = STEPS.index((0, 0))

    def row_of(k, i):
        along_x, along_y = [
            pick(k, [STEPS[n * BATCH + i][axis] for n in range(batches)]) for axis in range(2)
        ]
        return lax.rem(at_x + along_x, batches) * BATCH + lax.rem(at_y + along_y, BATCH)

    last = nper - 1

    def load(k, c, i):
        when = pl.ds(per - chunk * (c + 1), chunk)
        return pltpu.make_async_copy(
            trans_hbm.at[row_of(k, i), when], maps.at[k * BATCH + i, when], load_sem.at[k, c, i]
        )

    small = [
        pltpu.make_async_copy(src, dst, small_sem.at[i])
        for i, (src, dst) in enumerate(
            [(force_hbm, force), (term_hbm, term), (part_hbm, part), (share_hbm, share)]
        )
    ]
    for copy in small:
        copy.start()
    for c in range(4):
        for i in range(BATCH):
            load(0, c, i).start()

    square = (sec, sec)
    eye = lax.broadcasted_iota(jnp.int32, square, 0) == lax.broadcasted_iota(jnp.int32, square, 1)
    unit[...] = jnp.where(eye, 1.0, 0.0)
    top = lax.broadcasted_iota(jnp.int32, (16, sec), 0) == 0

    def upright(vector):
        return jnp.sum(jnp.where(eye, vector, 0.0), axis=1, keepdims=True)

    def move_map(slot, source, target):
        return [
            pltpu.make_async_remote_copy(
                src_ref=src.at[slot],
                dst_ref=dst.at[source],
                send_sem=send.at[slot],
                recv_sem=recv.at[source],
                device_id=(target, zone),
                device_id_type=MESH,
            )
            for src, dst, send, recv in [
                (outgoing, incoming, map_send, map_recv),
                (shifts, given, shift_send, shift_recv),
            ]
        ]

    def send_map(k, i):
        return move_map(k * BATCH + i, here, row_of(k, i))

    def keep_map():
        return [
            pltpu.make_async_copy(outgoing.at[own], incoming.at[here], map_recv.at[here]),
            pltpu.make_async_copy(shifts.at[own], given.at[here], shift_recv.at[here]),
        ]

    for copy in small[:2]:
        copy.wait()

    def compose(k, carry):
        @pl.when(k < batches - 1)
        def _():
            for c in range(4):
                for i in range(BATCH):
                    load(k + 1, c, i).start()

        for c in range(4):
            for i in range(BATCH):
                load(k, c, i).wait()
            for inner in range(chunk):
                t = per - 1 - chunk * c - inner
                for i in range(BATCH):
                    row, slot = row_of(k, i), k * BATCH + i
                    block = maps[slot, t]
                    source = force[row, t : t + 1]
                    if t == per - 1:
                        prod = block.T
                        offset = jnp.broadcast_to(source, (8, sec))
                    else:
                        high, low = split(block - unit[...])
                        late, late_offset = maps[slot, t + 1], offsets[slot, t + 1 : t + 2]
                        late_high, late_low = split(late)
                        tail_high, tail_low = split(jnp.where(top, late_offset, 0.0))
                        tall_high = jnp.concatenate([late_high, tail_high], 0)
                        tall_low = jnp.concatenate([late_low, tail_low], 0)
                        prod = dot(
                            jnp.concatenate([tall_high, tall_low, tall_high], 1),
                            jnp.concatenate([high, high, low], 1),
                            NT,
                        )
                        offset = prod[sec : sec + 8] + late_offset + source
                        prod = prod[:sec] + late
                    maps[slot, t] = prod
                    offsets[slot, t : t + 1] = offset[:1]
                    if t == 0:
                        outgoing[slot] = prod
                        shifts[slot] = offset[:1]

        @pl.when(k == 0)
        def _():
            pl.semaphore_wait(barrier, nper + nreg - 2)

        @pl.when(here == last)
        def _():
            for i in range(BATCH):
                slot = k * BATCH + i
                column = upright(term[pl.ds(row_of(k, i), 1), :])
                value = jnp.sum(maps[slot, 0] * column, axis=0, keepdims=True)
                shifts[slot] = value + offsets[slot, 0:1]

        for i in range(BATCH):
            row = row_of(k, i)

            @pl.when((row != here) & (here != 0))
            def _(i=i):
                send_map(k, i)[1].start()

            @pl.when((row != here) & (here != 0) & (here != last))
            def _(i=i):
                send_map(k, i)[0].start()

            @pl.when((row == here) & (here != 0))
            def _():
                keep_map()[1].start()

            @pl.when((row == here) & (here != 0) & (here != last))
            def _():
                keep_map()[0].start()

        return carry

    lax.fori_loop(0, batches, compose, 0)

    for copy in small[2:]:
        copy.wait()

    region = lax.broadcasted_iota(jnp.int32, square, 0)
    for g in range(BLOCKS):
        ids, amounts = part[g], share[g]
        trade = jnp.zeros(square, F32)
        for j in range(ids.shape[0]):
            trade += jnp.where(ids[j : j + 1] == region, amounts[j : j + 1], 0.0)
        high, low = split(trade.T)
        side = sec * (g % 2)
        mixer[g // 2, :sec, side : side + sec] = high
        mixer[g // 2, sec:, side : side + sec] = low

    def send_edge(p):
        return pltpu.make_async_remote_copy(
            src_ref=edges.at[p],
            dst_ref=starts.at[here],
            send_sem=edge_send.at[p],
            recv_sem=edge_recv.at[here],
            device_id=(p, zone),
            device_id_type=MESH,
        )

    def keep_edge():
        return pltpu.make_async_copy(edges.at[here], starts.at[here], edge_recv.at[here])

    def ship_edge(p):
        @pl.when(p != here)
        def _():
            send_edge(p).start()

        @pl.when(p == here)
        def _():
            keep_edge().start()

    edges[last] = term[pl.ds(here, 1), :]
    ship_edge(last)

    @pl.when(here != last)
    def _():
        move_map(last, last, last)[1].wait_recv()

    @pl.when(here == last)
    def _():
        keep_map()[1].wait()

    state = given[last]
    edges[last - 1] = state

    def chain(step, state):
        p = last - 1 - step

        @pl.when(p != here)
        def _():
            for copy in move_map(p, p, p):
                copy.wait_recv()

        @pl.when(p == here)
        def _():
            for copy in keep_map():
                copy.wait()

        ship_edge(p)
        moved = incoming[p] * upright(state)
        state = jnp.sum(moved, axis=0, keepdims=True) + given[p]
        edges[p - 1] = state
        return state

    lax.fori_loop(0, nper - 2, chain, state)
    ship_edge(0)

    def arrive(row, carry):
        @pl.when(row != here)
        def _():
            pltpu.make_async_remote_copy(
                src_ref=edges.at[row],
                dst_ref=starts.at[row],
                send_sem=edge_send.at[row],
                recv_sem=edge_recv.at[row],
                device_id=(row, zone),
                device_id_type=MESH,
            ).wait_recv()

        @pl.when(row == here)
        def _():
            keep_edge().wait()

        return carry

    lax.fori_loop(0, rows, arrive, 0)
    for k in range(batches):
        for i in range(BATCH):
            column = upright(starts[row_of(k, i)])
            columns[k * BATCH + i] = jnp.broadcast_to(column, square)

    def send_flow(other):
        return pltpu.make_async_remote_copy(
            src_ref=flow.at[pl.ds(other * share_t, share_t)],
            dst_ref=traded.at[:, pl.ds(pl.multiple_of(zone * rows, 8), rows)],
            send_sem=flow_send.at[other],
            recv_sem=flow_recv.at[zone],
            device_id=(here, other),
            device_id_type=MESH,
        )

    def keep_flow():
        return pltpu.make_async_copy(
            flow.at[pl.ds(zone * share_t, share_t)],
            traded.at[:, pl.ds(pl.multiple_of(zone * rows, 8), rows)],
            flow_recv.at[zone],
        )

    def got_flow(other):
        return pltpu.make_async_remote_copy(
            src_ref=flow.at[pl.ds(other * share_t, share_t)],
            dst_ref=traded.at[:, pl.ds(pl.multiple_of(other * rows, 8), rows)],
            send_sem=flow_send.at[other],
            recv_sem=flow_recv.at[other],
            device_id=(here, other),
            device_id_type=MESH,
        )

    layers = nreg // 2
    order = [(dz, dc) for dz in (2, 1, 3, 0) if dz < layers for dc in (1, 0)]
    others = []
    for dz, dc in order:
        other = lax.rem(lax.div(zone, 2) + dz, layers) * 2 + lax.rem(zone + dc, 2)
        for step in range(share_t):
            t = other * share_t + step
            for k in range(batches):
                for i in range(BATCH):
                    slot, row = k * BATCH + i, row_of(k, i)
                    value = jnp.sum(maps[slot, t] * columns[slot], axis=0, keepdims=True)
                    value += offsets[slot, pl.ds(t, 1), :]
                    costate[row, pl.ds(t, 1), :] = value
                    flow[t, pl.ds(row, 1), :] = value
            flow[t] = jnp.tanh(flow[t])
        if (dz, dc) != (0, 0):
            others.append(other)
            send_flow(other).start()
        else:
            keep_flow().start()

    def drain(row, carry):
        @pl.when(row != here)
        def _():
            send_edge(row).wait_send()

        @pl.when((row != own) & (here != 0))
        def _():
            move_map(row, here, row)[1].wait_send()

        @pl.when((row != own) & (here != 0) & (here != last))
        def _():
            move_map(row, here, row)[0].wait_send()

        return carry

    lax.fori_loop(0, rows, drain, 0)

    keep_flow().wait()
    for other in others:
        got_flow(other).wait_recv()
    for other in others:
        send_flow(other).wait_send()


def mix(traded, mixer, costate, costate_hbm, clear_hbm, clear, out_sem):
    share_t, sec = traded.shape[0], traded.shape[2]
    save = pltpu.make_async_copy(costate, costate_hbm, out_sem.at[0])
    save.start()
    width = share_t * sec
    whole = jnp.concatenate([traded[t] for t in range(share_t)], 1)
    high, low = split(whole)
    group = lax.div(
        lax.rem(lax.broadcasted_iota(jnp.int32, (1, width), 1), sec), sec // BLOCKS
    )
    mixed = jnp.zeros((sec, width), F32)
    for pair in range(BLOCKS // 2):
        masks = [group == 2 * pair, group == 2 * pair + 1]
        tall_high = jnp.concatenate([jnp.where(m, high, BF16(0)) for m in masks], 0)
        tall_low = jnp.concatenate([jnp.where(m, low, BF16(0)) for m in masks], 0)
        first = dot(mixer[pair], tall_high, NN)
        mixed += first[:sec] + first[sec:]
        mixed += dot(mixer[pair, :sec], tall_low, NN)
    result = whole - mixed
    for t in range(share_t):
        clear[:, t, :] = result[:, t * sec : (t + 1) * sec]
    done = pltpu.make_async_copy(clear, clear_hbm, out_sem.at[1])
    done.start()
    save.wait()
    done.wait()


def shards(nper, nreg, transition, forcing, terminal, partners, shares):
    rows, per, sec = forcing.shape
    regions = partners.shape[1]
    share_t = per // nreg
    ids, amounts = jnp.swapaxes(partners, 1, 2), jnp.swapaxes(shares, 1, 2)
    anywhere = pl.BlockSpec(memory_space=pl.ANY)
    local = pl.BlockSpec(memory_space=pltpu.VMEM)
    dma = pltpu.SemaphoreType.DMA
    costate, traded, mixer = pl.pallas_call(
        functools.partial(kernel, nper, nreg),
        out_shape=(
            pltpu.VMEM((rows, per, sec), F32),
            pltpu.VMEM((share_t, regions, sec), F32),
            pltpu.VMEM((BLOCKS // 2, 2 * regions, 2 * regions), BF16),
        ),
        in_specs=[anywhere] * 5,
        out_specs=[local] * 3,
        scratch_shapes=[
            pltpu.VMEM((rows, per, sec, sec), F32),
            pltpu.VMEM((rows, per, sec), F32),
            pltpu.VMEM((rows, sec), F32),
            pltpu.VMEM(ids.shape, jnp.int32),
            pltpu.VMEM(amounts.shape, F32),
            pltpu.VMEM((rows, per, sec), F32),
            pltpu.VMEM((sec, sec), F32),
            pltpu.VMEM((rows, sec, sec), F32),
            pltpu.VMEM((nper, sec, sec), F32),
            pltpu.VMEM((rows, 1, sec), F32),
            pltpu.VMEM((nper, 1, sec), F32),
            pltpu.VMEM((nper, 1, sec), F32),
            pltpu.VMEM((rows, 1, sec), F32),
            pltpu.VMEM((rows, sec, sec), F32),
            pltpu.VMEM((per, rows, sec), F32),
            dma((rows // BATCH, 4, BATCH)),
            dma((4,)),
            dma((rows,)),
            dma((nper,)),
            dma((rows,)),
            dma((nper,)),
            dma((nper,)),
            dma((rows,)),
            dma((nreg,)),
            dma((nreg,)),
        ],
        compiler_params=pltpu.CompilerParams(
            collective_id=0, has_side_effects=True, vmem_limit_bytes=60 * 2**20
        ),
        name="newton_step",
    )(transition, forcing, terminal, ids, amounts)
    return pl.pallas_call(
        mix,
        out_shape=(
            jax.ShapeDtypeStruct((rows, per, sec), F32),
            jax.ShapeDtypeStruct((regions, share_t, sec), F32),
        ),
        in_specs=[local] * 3,
        out_specs=[anywhere] * 2,
        scratch_shapes=[pltpu.VMEM((regions, share_t, sec), F32), dma((2,))],
        compiler_params=pltpu.CompilerParams(vmem_limit_bytes=8 * 2**20),
        name="trade_mix",
    )(traded, mixer, costate)


def solution(mesh):
    return jax.shard_map(
        functools.partial(shards, mesh.shape["period"], mesh.shape["region"]),
        mesh=mesh,
        in_specs=(
            P("region", "period", None, None),
            P("region", "period", None),
            P("region", None),
            P(),
            P(),
        ),
        out_specs=(P("region", "period", None), P(None, ("period", "region"), None)),
        check_vma=False,
    )
```

```python
import functools

import jax
import jax.numpy as jnp
from jax import lax
from jax.experimental import pallas as pl
from jax.experimental.pallas import tpu as pltpu
from jax.sharding import PartitionSpec as P

BLOCKS = 8
BATCH = 4
STEPS = (
    ((2, 2), (2, 1), (1, 2), (2, 3))
    + ((3, 2), (2, 0), (0, 2), (1, 1))
    + ((3, 3), (1, 3), (3, 1), (0, 3))
    + ((0, 1), (1, 0), (3, 0), (0, 0))
)
NT = (((1,), (1,)), ((), ()))
NN = (((1,), (0,)), ((), ()))
F32 = jnp.float32
BF16 = jnp.bfloat16
MESH = pl.DeviceIdType.MESH


def split(x):
    high = x.astype(BF16)
    return high, (x - high.astype(F32)).astype(BF16)


def dot(left, right, dims):
    return lax.dot_general(left, right, dims, preferred_element_type=F32)


def kernel(
    nper,
    nreg,
    trans_hbm,
    force_hbm,
    term_hbm,
    part_hbm,
    share_hbm,
    costate,
    traded,
    mixer,
    maps,
    force,
    term,
    part,
    share,
    offsets,
    unit,
    outgoing,
    incoming,
    shifts,
    given,
    edges,
    starts,
    columns,
    flow,
    load_sem,
    small_sem,
    map_send,
    map_recv,
    shift_send,
    shift_recv,
    edge_send,
    edge_recv,
    flow_send,
    flow_recv,
):
    rows, per, sec = force.shape
    here, zone = lax.axis_index("period"), lax.axis_index("region")
    batches = rows // BATCH
    chunk = per // 4
    share_t = per // nreg

    barrier = pltpu.get_barrier_semaphore()
    for step in range(1, nper):
        pl.semaphore_signal(
            barrier, inc=1, device_id=(lax.rem(here + step, nper), zone), device_id_type=MESH
        )
    for step in range(1, nreg):
        pl.semaphore_signal(
            barrier, inc=1, device_id=(here, lax.rem(zone + step, nreg)), device_id_type=MESH
        )

    def pick(k, table):
        found = table[-1]
        for n, entry in enumerate(table[:-1]):
            found = jnp.where(k == n, entry, found)
        return found

    at_x, at_y = lax.div(here, BATCH), lax.rem(here, BATCH)
    own = STEPS.index((0, 0))

    def row_of(k, i):
        along_x, along_y = [
            pick(k, [STEPS[n * BATCH + i][axis] for n in range(batches)]) for axis in range(2)
        ]
        return lax.rem(at_x + along_x, batches) * BATCH + lax.rem(at_y + along_y, BATCH)

    last = nper - 1

    def load(k, c, i):
        when = pl.ds(per - chunk * (c + 1), chunk)
        return pltpu.make_async_copy(
            trans_hbm.at[row_of(k, i), when], maps.at[k * BATCH + i, when], load_sem.at[k, c, i]
        )

    small = [
        pltpu.make_async_copy(src, dst, small_sem.at[i])
        for i, (src, dst) in enumerate(
            [(force_hbm, force), (term_hbm, term), (part_hbm, part), (share_hbm, share)]
        )
    ]
    for copy in small:
        copy.start()
    for c in range(4):
        for i in range(BATCH):
            load(0, c, i).start()

    square = (sec, sec)
    eye = lax.broadcasted_iota(jnp.int32, square, 0) == lax.broadcasted_iota(jnp.int32, square, 1)
    unit[...] = jnp.where(eye, 1.0, 0.0)
    top = lax.broadcasted_iota(jnp.int32, (16, sec), 0) == 0

    def upright(vector):
        return jnp.sum(jnp.where(eye, vector, 0.0), axis=1, keepdims=True)

    def move_map(slot, source, target):
        return [
            pltpu.make_async_remote_copy(
                src_ref=src.at[slot],
                dst_ref=dst.at[source],
                send_sem=send.at[slot],
                recv_sem=recv.at[source],
                device_id=(target, zone),
                device_id_type=MESH,
            )
            for src, dst, send, recv in [
                (outgoing, incoming, map_send, map_recv),
                (shifts, given, shift_send, shift_recv),
            ]
        ]

    def send_map(k, i):
        return move_map(k * BATCH + i, here, row_of(k, i))

    def keep_map():
        return [
            pltpu.make_async_copy(outgoing.at[own], incoming.at[here], map_recv.at[here]),
            pltpu.make_async_copy(shifts.at[own], given.at[here], shift_recv.at[here]),
        ]

    for copy in small[:2]:
        copy.wait()

    def compose(k, carry):
        for c in range(4):
            for i in range(BATCH):
                load(k, c, i).wait()

            if c == 0:

                @pl.when(k < batches - 1)
                def _():
                    for later in range(4):
                        for i in range(BATCH):
                            load(k + 1, later, i).start()

            for inner in range(chunk):
                t = per - 1 - chunk * c - inner
                for i in range(BATCH):
                    row, slot = row_of(k, i), k * BATCH + i
                    block = maps[slot, t]
                    source = force[row, t : t + 1]
                    if t == per - 1:
                        prod = block.T
                        offset = jnp.broadcast_to(source, (8, sec))
                    else:
                        high, low = split(block - unit[...])
                        late, late_offset = maps[slot, t + 1], offsets[slot, t + 1 : t + 2]
                        late_high, late_low = split(late)
                        tail_high, tail_low = split(jnp.where(top, late_offset, 0.0))
                        tall_high = jnp.concatenate([late_high, tail_high], 0)
                        tall_low = jnp.concatenate([late_low, tail_low], 0)
                        prod = dot(
                            jnp.concatenate([tall_high, tall_low, tall_high], 1),
                            jnp.concatenate([high, high, low], 1),
                            NT,
                        )
                        offset = prod[sec : sec + 8] + late_offset + source
                        prod = prod[:sec] + late
                    maps[slot, t] = prod
                    offsets[slot, t : t + 1] = offset[:1]
                    if t == 0:
                        outgoing[slot] = prod
                        shifts[slot] = offset[:1]

        @pl.when(k == 0)
        def _():
            pl.semaphore_wait(barrier, nper + nreg - 2)

        @pl.when(here == last)
        def _():
            for i in range(BATCH):
                slot = k * BATCH + i
                column = upright(term[pl.ds(row_of(k, i), 1), :])
                value = jnp.sum(maps[slot, 0] * column, axis=0, keepdims=True)
                shifts[slot] = value + offsets[slot, 0:1]

        for i in range(BATCH):
            row = row_of(k, i)

            @pl.when((row != here) & (here != 0))
            def _(i=i):
                send_map(k, i)[1].start()

            @pl.when((row != here) & (here != 0) & (here != last))
            def _(i=i):
                send_map(k, i)[0].start()

            @pl.when((row == here) & (here != 0))
            def _():
                keep_map()[1].start()

            @pl.when((row == here) & (here != 0) & (here != last))
            def _():
                keep_map()[0].start()

        return carry

    lax.fori_loop(0, batches, compose, 0)

    for copy in small[2:]:
        copy.wait()

    region = lax.broadcasted_iota(jnp.int32, square, 0)
    for g in range(BLOCKS):
        ids, amounts = part[g], share[g]
        trade = jnp.zeros(square, F32)
        for j in range(ids.shape[0]):
            trade += jnp.where(ids[j : j + 1] == region, amounts[j : j + 1], 0.0)
        high, low = split(trade.T)
        side = sec * (g % 2)
        mixer[g // 2, :sec, side : side + sec] = high
        mixer[g // 2, sec:, side : side + sec] = low

    def send_edge(p):
        return pltpu.make_async_remote_copy(
            src_ref=edges.at[p],
            dst_ref=starts.at[here],
            send_sem=edge_send.at[p],
            recv_sem=edge_recv.at[here],
            device_id=(p, zone),
            device_id_type=MESH,
        )

    def keep_edge():
        return pltpu.make_async_copy(edges.at[here], starts.at[here], edge_recv.at[here])

    def ship_edge(p):
        @pl.when(p != here)
        def _():
            send_edge(p).start()

        @pl.when(p == here)
        def _():
            keep_edge().start()

    edges[last] = term[pl.ds(here, 1), :]
    ship_edge(last)

    @pl.when(here != last)
    def _():
        move_map(last, last, last)[1].wait_recv()

    @pl.when(here == last)
    def _():
        keep_map()[1].wait()

    state = given[last]
    edges[last - 1] = state

    def chain(step, state):
        p = last - 1 - step
        ship_edge(p)

        @pl.when(p != here)
        def _():
            for copy in move_map(p, p, p):
                copy.wait_recv()

        @pl.when(p == here)
        def _():
            for copy in keep_map():
                copy.wait()

        moved = incoming[p] * upright(state)
        state = jnp.sum(moved, axis=0, keepdims=True) + given[p]
        edges[p - 1] = state
        return state

    lax.fori_loop(0, nper - 2, chain, state)
    ship_edge(0)

    def arrive(row, carry):
        @pl.when(row != here)
        def _():
            pltpu.make_async_remote_copy(
                src_ref=edges.at[row],
                dst_ref=starts.at[row],
                send_sem=edge_send.at[row],
                recv_sem=edge_recv.at[row],
                device_id=(row, zone),
                device_id_type=MESH,
            ).wait_recv()

        @pl.when(row == here)
        def _():
            keep_edge().wait()

        return carry

    lax.fori_loop(0, rows, arrive, 0)
    for k in range(batches):
        for i in range(BATCH):
            column = upright(starts[row_of(k, i)])
            columns[k * BATCH + i] = jnp.broadcast_to(column, square)

    def send_flow(other):
        return pltpu.make_async_remote_copy(
            src_ref=flow.at[pl.ds(other * share_t, share_t)],
            dst_ref=traded.at[:, pl.ds(pl.multiple_of(zone * rows, 8), rows)],
            send_sem=flow_send.at[other],
            recv_sem=flow_recv.at[zone],
            device_id=(here, other),
            device_id_type=MESH,
        )

    def keep_flow():
        return pltpu.make_async_copy(
            flow.at[pl.ds(zone * share_t, share_t)],
            traded.at[:, pl.ds(pl.multiple_of(zone * rows, 8), rows)],
            flow_recv.at[zone],
        )

    def got_flow(other):
        return pltpu.make_async_remote_copy(
            src_ref=flow.at[pl.ds(other * share_t, share_t)],
            dst_ref=traded.at[:, pl.ds(pl.multiple_of(other * rows, 8), rows)],
            send_sem=flow_send.at[other],
            recv_sem=flow_recv.at[other],
            device_id=(here, other),
            device_id_type=MESH,
        )

    layers = nreg // 2
    order = [(dz, dc) for dz in (2, 1, 3, 0) if dz < layers for dc in (1, 0)]
    others = []
    for dz, dc in order:
        other = lax.rem(lax.div(zone, 2) + dz, layers) * 2 + lax.rem(zone + dc, 2)
        for step in range(share_t):
            t = other * share_t + step
            for k in range(batches):
                for i in range(BATCH):
                    slot, row = k * BATCH + i, row_of(k, i)
                    value = jnp.sum(maps[slot, t] * columns[slot], axis=0, keepdims=True)
                    value += offsets[slot, pl.ds(t, 1), :]
                    costate[row, pl.ds(t, 1), :] = value
                    flow[t, pl.ds(row, 1), :] = value
            flow[t] = jnp.tanh(flow[t])
        if (dz, dc) != (0, 0):
            others.append(other)
            send_flow(other).start()
        else:
            keep_flow().start()

    def drain(row, carry):
        @pl.when(row != here)
        def _():
            send_edge(row).wait_send()

        @pl.when((row != own) & (here != 0))
        def _():
            move_map(row, here, row)[1].wait_send()

        @pl.when((row != own) & (here != 0) & (here != last))
        def _():
            move_map(row, here, row)[0].wait_send()

        return carry

    lax.fori_loop(0, rows, drain, 0)

    keep_flow().wait()
    for other in others:
        got_flow(other).wait_recv()
    for other in others:
        send_flow(other).wait_send()


def mix(traded, mixer, costate, costate_hbm, clear_hbm, clear, out_sem):
    share_t, sec = traded.shape[0], traded.shape[2]
    save = pltpu.make_async_copy(costate, costate_hbm, out_sem.at[0])
    save.start()
    width = share_t * sec
    whole = jnp.concatenate([traded[t] for t in range(share_t)], 1)
    high, low = split(whole)
    group = lax.div(
        lax.rem(lax.broadcasted_iota(jnp.int32, (1, width), 1), sec), sec // BLOCKS
    )
    mixed = jnp.zeros((sec, width), F32)
    for pair in range(BLOCKS // 2):
        masks = [group == 2 * pair, group == 2 * pair + 1]
        tall_high = jnp.concatenate([jnp.where(m, high, BF16(0)) for m in masks], 0)
        tall_low = jnp.concatenate([jnp.where(m, low, BF16(0)) for m in masks], 0)
        first = dot(mixer[pair], tall_high, NN)
        mixed += first[:sec] + first[sec:]
        mixed += dot(mixer[pair, :sec], tall_low, NN)
    result = whole - mixed
    for t in range(share_t):
        clear[:, t, :] = result[:, t * sec : (t + 1) * sec]
    done = pltpu.make_async_copy(clear, clear_hbm, out_sem.at[1])
    done.start()
    save.wait()
    done.wait()


def shards(nper, nreg, transition, forcing, terminal, partners, shares):
    rows, per, sec = forcing.shape
    regions = partners.shape[1]
    share_t = per // nreg
    ids, amounts = jnp.swapaxes(partners, 1, 2), jnp.swapaxes(shares, 1, 2)
    anywhere = pl.BlockSpec(memory_space=pl.ANY)
    local = pl.BlockSpec(memory_space=pltpu.VMEM)
    dma = pltpu.SemaphoreType.DMA
    costate, traded, mixer = pl.pallas_call(
        functools.partial(kernel, nper, nreg),
        out_shape=(
            pltpu.VMEM((rows, per, sec), F32),
            pltpu.VMEM((share_t, regions, sec), F32),
            pltpu.VMEM((BLOCKS // 2, 2 * regions, 2 * regions), BF16),
        ),
        in_specs=[anywhere] * 5,
        out_specs=[local] * 3,
        scratch_shapes=[
            pltpu.VMEM((rows, per, sec, sec), F32),
            pltpu.VMEM((rows, per, sec), F32),
            pltpu.VMEM((rows, sec), F32),
            pltpu.VMEM(ids.shape, jnp.int32),
            pltpu.VMEM(amounts.shape, F32),
            pltpu.VMEM((rows, per, sec), F32),
            pltpu.VMEM((sec, sec), F32),
            pltpu.VMEM((rows, sec, sec), F32),
            pltpu.VMEM((nper, sec, sec), F32),
            pltpu.VMEM((rows, 1, sec), F32),
            pltpu.VMEM((nper, 1, sec), F32),
            pltpu.VMEM((nper, 1, sec), F32),
            pltpu.VMEM((rows, 1, sec), F32),
            pltpu.VMEM((rows, sec, sec), F32),
            pltpu.VMEM((per, rows, sec), F32),
            dma((rows // BATCH, 4, BATCH)),
            dma((4,)),
            dma((rows,)),
            dma((nper,)),
            dma((rows,)),
            dma((nper,)),
            dma((nper,)),
            dma((rows,)),
            dma((nreg,)),
            dma((nreg,)),
        ],
        compiler_params=pltpu.CompilerParams(
            collective_id=0, has_side_effects=True, vmem_limit_bytes=60 * 2**20
        ),
        name="newton_step",
    )(transition, forcing, terminal, ids, amounts)
    return pl.pallas_call(
        mix,
        out_shape=(
            jax.ShapeDtypeStruct((rows, per, sec), F32),
            jax.ShapeDtypeStruct((regions, share_t, sec), F32),
        ),
        in_specs=[local] * 3,
        out_specs=[anywhere] * 2,
        scratch_shapes=[pltpu.VMEM((regions, share_t, sec), F32), dma((2,))],
        compiler_params=pltpu.CompilerParams(vmem_limit_bytes=8 * 2**20),
        name="trade_mix",
    )(traded, mixer, costate)


def solution(mesh):
    return jax.shard_map(
        functools.partial(shards, mesh.shape["period"], mesh.shape["region"]),
        mesh=mesh,
        in_specs=(
            P("region", "period", None, None),
            P("region", "period", None),
            P("region", None),
            P(),
            P(),
        ),
        out_specs=(P("region", "period", None), P(None, ("period", "region"), None)),
        check_vma=False,
    )
```
